32 devices in a mesh: groups: 1, expert: 8 (over z, y), tensor: 2 (over x), pair: 2 (over core).
Axes of the slice: x: 2, y: 2, z: 4, core: 2. Of those that a mesh axis runs over, the one named last changes fastest.
Arguments:
- tokens: bfloat16 [512, 3584], P(('groups', 'expert', 'tensor', 'pair')), may hold values from -6 to 6
- expert_ids: int32 [512, 8], P(('groups', 'expert', 'tensor', 'pair')), may hold values from 0 to 15, all different within a row; in each aligned block of 16 rows (0 to 15, 16 to 31, ...) at most 16 rows name the same one
- route_weight: float32 [512, 8], P(('groups', 'expert', 'tensor', 'pair')), may hold values from 0.05 to 0.5
- w_gate: bfloat16 [16, 3584, 1024], P(('expert', 'pair'), None, 'tensor'), may hold values from -0.09375 to 0.09375
- w_up: bfloat16 [16, 3584, 1024], P(('expert', 'pair'), None, 'tensor'), may hold values from -0.09375 to 0.09375
- w_down: bfloat16 [16, 1024, 3584], P(('expert', 'pair'), 'tensor'), may hold values from -0.1875 to 0.1875
- s_gate: bfloat16 [3584, 2048], P(None, ('tensor', 'pair')), may hold values from -0.09375 to 0.09375
- s_up: bfloat16 [3584, 2048], P(None, ('tensor', 'pair')), may hold values from -0.09375 to 0.09375
- s_down: bfloat16 [2048, 3584], P(('tensor', 'pair')), may hold values from -0.125 to 0.125
Outputs:
- moe_out: bfloat16 [512, 3584], P(('groups', 'expert', 'tensor', 'pair'))
The draws below stay inside these ranges and needn't reach their ends.
Inputs may be any that keep to these rules, and one draw needn't show every extreme that they name: `expert_ids`: each row names 8 different experts. Among the 16 tokens of one device no expert is named by more than 16 tokens, and in every draw some expert is named by exactly 16 tokens of some device.
All inputs are finite; a program needn't handle non-finite values.
Results may differ from the reference program's by a relative error of at most 0.014.
Values may be sent and summed in bfloat16 or wider, within the bound.
A program may use at most 64 MiB of HBM per device.

```python
import math
import jax
import jax.numpy as jnp
import numpy as np
from jax import lax

D = 3584
EH = 1024
SH = 2048
TOP = 8
TOK_DEV = 16
EXPERTS = 16
CAP = 16
TOKENS = 512
N_EXPERT = 8
N_TENSOR = 2
N_PAIR = 2


def block_levels(key, dims, cuts, smallest, largest):
    level, own = 1.0, jax.random.fold_in(key, 6)
    for dim, parts in cuts:
        steps = jnp.exp(jax.random.uniform(jax.random.fold_in(own, dim), (parts,), jnp.float32, smallest / len(cuts), largest / len(cuts)))
        level = level * jnp.repeat(steps, dims[dim] // parts).reshape([-1 if axis == dim else 1 for axis in range(len(dims))])
    return level


def routed_block(rng, own, number, rows, amount, top, bound, slope):
    ranking = jax.random.permutation(rng, amount)
    heavy_load, ordinary = portions_of(amount, rows * top, bound, slope, True), portions_of(amount, rows * top, bound, slope, False)
    places = jnp.arange(amount)

    def named(lengths, turn):
        used = int((lengths > 0).sum())
        fixed = max(1, used // 4)
        passed = fixed + (places - fixed + turn * (used - fixed)) % max(1, amount - fixed)
        return jnp.zeros((amount,), jnp.int32).at[ranking[jnp.where(places < fixed, places, passed)]].set(jnp.asarray(lengths, jnp.int32))

    lengths = jnp.where(number % 4 == 0, named(heavy_load, number // 4), named(ordinary, number - number // 4 - 1))
    mixed = jax.random.permutation(jax.random.fold_in(own, 3), amount)
    donor, sink = mixed[0:amount // 2 * 2:2], mixed[1:amount // 2 * 2:2]
    room = jnp.minimum(lengths[donor] - 1, bound - lengths[sink]) // 2
    room = jnp.where((donor == ranking[0]) | (sink == ranking[0]) | (lengths[sink] == 0), 0, jnp.maximum(room, 0))
    passed = jax.random.randint(jax.random.fold_in(own, 4), (amount // 2,), 0, 1 << 20) % (room + 1)
    lengths = lengths.at[donor].add(-passed).at[sink].add(passed)
    items = jnp.searchsorted(jnp.cumsum(lengths), jnp.arange(rows * top), side="right").astype(jnp.int32)
    grid = items.reshape(top, rows).T
    grid = grid[jax.random.permutation(jax.random.fold_in(own, 1), rows)]
    turn = jax.random.randint(jax.random.fold_in(own, 2), (rows, 1), 0, top)
    return jnp.take_along_axis(grid, (jnp.arange(top)[None, :] + turn) % top, axis=1)


def portions_of(count, total, limit, lean, full):
    weights = [(1 << 20) // math.isqrt(standing ** lean) + 1 for standing in range(1, count + 1)]
    largest = limit if full else min(limit, max(-(-total // count), total * weights[0] // sum(weights)))
    least = 1 if total - largest >= count - 1 else 0
    holding, surplus = [largest] + [least] * (count - 1), total - largest - least * (count - 1)
    while surplus > 0:
        candidates = [i for i in range(1, count) if holding[i] < largest] or [i for i in range(1, count) if holding[i] < limit]
        mass, left = sum([weights[i] for i in candidates]), surplus
        for i in candidates:
            addition = min(limit - holding[i], max(1, left * weights[i] // mass), surplus)
            holding[i] = holding[i] + addition
            surplus = surplus - addition
    return np.array(holding)


def centred(own_key, shape, scale, limit, cuts=(), kind=jnp.bfloat16):
    values = scale * jax.random.normal(own_key, shape, jnp.float32)
    if cuts:
        values = values * block_levels(own_key, shape, cuts, -0.22, 0.18)
    return jnp.clip(values, -limit, limit).astype(kind)


def setup_inputs(seed: int = 0, part: int = 0) -> dict:
    key_of = jax.random.split(jax.random.key(seed), 10)
    part_splits = jax.random.split(jax.random.fold_in(key_of[9], part), 10)
    tokens = centred(part_splits[0], (TOKENS, D), 1.0, 6.0, ((0, 32),))
    expert_ids_keys = jax.random.split(jax.random.fold_in(part_splits[1], 1), TOKENS // TOK_DEV)
    expert_ids_turns = jax.random.permutation(jax.random.fold_in(part_splits[1], 3), TOKENS // TOK_DEV)
    expert_ids = jax.vmap(lambda own, number: routed_block(jax.random.fold_in(part_splits[1], 2), own, number, TOK_DEV, EXPERTS, TOP, CAP, 2))(expert_ids_keys, expert_ids_turns).reshape((TOKENS, TOP))
    route_weight = jnp.clip(0.05 + 0.45 * jax.random.uniform(part_splits[2], (TOKENS, TOP), jnp.float32) ** block_levels(part_splits[2], (TOKENS, TOP), ((0, 32),), -0.2, 0.2), 0.05, 0.5)
    w_gate = centred(key_of[3], (EXPERTS, D, EH), D ** -0.5, 0.09375, ((0, 16), (2, 2)))
    w_up = centred(key_of[4], (EXPERTS, D, EH), D ** -0.5, 0.09375, ((0, 16), (2, 2)))
    w_down = centred(key_of[5], (EXPERTS, EH, D), EH ** -0.5, 0.1875, ((0, 16), (1, 2)))
    s_gate = centred(key_of[6], (D, SH), D ** -0.5, 0.09375, ((1, 4),))
    s_up = centred(key_of[7], (D, SH), D ** -0.5, 0.09375, ((1, 4),))
    s_down = centred(key_of[8], (SH, D), SH ** -0.5, 0.125, ((0, 4),))
    return dict(tokens=tokens, expert_ids=expert_ids, route_weight=route_weight, w_gate=w_gate, w_up=w_up, w_down=w_down, s_gate=s_gate, s_up=s_up, s_down=s_down)


def reference(tokens, expert_ids, route_weight, w_gate, w_up, w_down, s_gate, s_up, s_down):
    highest = lax.Precision.HIGHEST
    tokens_wide = tokens.astype(jnp.float32)
    shared_gate = jnp.dot(tokens_wide, s_gate.astype(jnp.float32), precision=highest)
    shared_upper = jnp.dot(tokens_wide, s_up.astype(jnp.float32), precision=highest)
    shared_hidden = (jax.nn.silu(shared_gate) * shared_upper).astype(jnp.bfloat16)
    shared_hidden = lax.optimization_barrier(shared_hidden).astype(jnp.float32)
    shared = jnp.dot(shared_hidden, s_down.astype(jnp.float32), precision=highest)
    rows_most = min(TOKENS, N_EXPERT * N_TENSOR * N_PAIR * CAP)
    slice_width = EH // N_TENSOR

    def expert_step(total, expert):
        matches = expert_ids == expert
        coefficient = jnp.sum(jnp.where(matches, route_weight, 0.0), axis=1)
        chosen = jnp.any(matches, axis=1)
        row_order = jnp.argsort(jnp.where(chosen, 0, 1).astype(jnp.int32), stable=True)[:rows_most].astype(jnp.int32)
        picked = tokens_wide[row_order]
        gate_part = jnp.dot(picked, w_gate[expert].astype(jnp.float32), precision=highest)
        upper_part = jnp.dot(picked, w_up[expert].astype(jnp.float32), precision=highest)
        hidden = (jax.nn.silu(gate_part) * upper_part).astype(jnp.bfloat16)
        hidden = lax.optimization_barrier(hidden).astype(jnp.float32)
        down_rows = w_down[expert].astype(jnp.float32).reshape(N_TENSOR, slice_width, D)
        pieces = jnp.einsum("rjh,jhd->jrd", hidden.reshape(rows_most, N_TENSOR, slice_width), down_rows, precision=highest)
        pieces = lax.optimization_barrier(pieces.astype(jnp.bfloat16)).astype(jnp.float32)
        result = lax.optimization_barrier(jnp.sum(pieces, axis=0).astype(jnp.bfloat16)).astype(jnp.float32)
        total = total.at[row_order].add(result * coefficient[row_order][:, None])
        return total, None

    routed, _ = lax.scan(expert_step, jnp.zeros((TOKENS, D), jnp.float32), jnp.arange(EXPERTS, dtype=jnp.int32))
    return (shared + routed).astype(jnp.bfloat16)
```

```python
import functools

import jax
import jax.numpy as jnp
from jax import lax
from jax.experimental import pallas as pl
from jax.experimental.pallas import tpu as pltpu
from jax.sharding import PartitionSpec as P

MESH = pl.DeviceIdType.MESH
F32 = jnp.float32
BF16 = jnp.bfloat16


def lanes_for(experts):
    return -(-3 * experts // 128) * 128


def tile_of(width, most):
    for tile in range(min(width, most), 0, -1):
        if width % tile == 0 and (tile % 128 == 0 or tile == width):
            return tile
    return width


class Layout:
    def __init__(self, n_expert, n_tensor, tok_rows, width, experts):
        self.nt = n_tensor
        self.ny = 2 if n_expert % 2 == 0 else 1
        self.nz = n_expert // self.ny
        self.chips = self.ny * self.nt
        self.plane = 2 * self.chips
        self.blocks = self.nz * self.plane
        self.rows, self.width, self.extra = tok_rows, width, lanes_for(experts)
        cut = width // 256 * 128
        self.cols = [(0, cut), (cut, width - cut)]
        self.wide = [(0, cut), (cut, width - cut + self.extra)]
        self.first = (self.nt, self.ny)
        self.last = (self.ny, self.nt)

    def sequence(self, z):
        nz = self.nz
        m = jnp.minimum(z, nz - 1 - z)
        out = [z]
        for i in range(1, nz):
            near = z + (i + 1) // 2 if i % 2 else z - i // 2
            far = jnp.where(z <= nz - 1 - z, z + (i - m), z - (i - m))
            out.append(jnp.where(i <= 2 * m, near, far))
        return out


def schedule(nz):
    ops = [("A2", 0), ("A1", 1), ("A3", 0), ("W", 0), ("S", 0), ("U", 0), ("A2", 1)]
    for i in range(nz):
        ops.append(("D", i))
        if i + 2 < nz:
            ops.append(("A1", i + 2))
        if i + 1 < nz:
            ops += [("A3", i + 1)]
        if i >= 1:
            ops.append(("L", i - 1))
        if i + 1 < nz:
            ops += [("W", i + 1), ("U", i + 1)]
        if i + 2 < nz:
            ops.append(("A2", i + 2))
        if i >= 2:
            ops.append(("F", i - 2))
        if i >= 3:
            ops.append(("Z", i - 3))
    rest = [("L", nz - 1), ("F", nz - 2), ("Z", nz - 3), ("F", nz - 1), ("Z", nz - 2), ("Z", nz - 1)]
    return ops + [op for op in rest if op[1] >= 0]


def kernel(lay, experts, tok_in, ids_in, rw_in, wg_in, wu_in, wd_in, sg_in, su_in, sd_in, out,
           tok, part, ids, rw, recvp, recvb0, recvb1, recva0, recva1, recvz, hid, hs,
           wg, wu, wd, sg, su, sd, load_sem, tok_send, tok_recv, red_send, pair_recv, b_recv, a_recv, z_recv):
    nz, ny, nt = lay.nz, lay.ny, lay.nt
    rows, width, chips = lay.rows, lay.width, lay.chips
    e_idx, t, p = lax.axis_index("expert"), lax.axis_index("tensor"), lax.axis_index("pair")
    z, y = e_idx // ny, e_idx % ny
    other = 1 - p
    seq = lay.sequence(z)

    def device(z_, y_, t_):
        return {"expert": z_ * ny + y_, "tensor": t_, "pair": p}

    partner = {"expert": e_idx, "tensor": t, "pair": other}
    t_peers = [(t + d) % nt for d in range(1, nt)]
    y_peers = [(y + d) % ny for d in range(1, ny)]

    barrier = pltpu.get_barrier_semaphore()

    def greet(dev):
        pl.semaphore_signal(barrier, inc=1, device_id=dev, device_id_type=MESH)

    for d in range(1, nz):
        greet(device((z + d) % nz, y, t))
    for t_ in t_peers:
        greet(device(z, y, t_))
    for y_ in y_peers:
        greet(device(z, y_, t))
    greet(partner)

    def place(q, z_, y_, t_):
        return ((z_ * 2 + q) * ny + y_) * nt + t_

    cols = [pl.ds(a, n) for a, n in lay.cols]
    wide = [pl.ds(a, n) for a, n in lay.wide]
    slices = range(len(cols))
    first_peers, last_peers = (t_peers, y_peers), (y_peers, t_peers)
    first_at, last_at = (t, y), (y, t)

    def yt(h, first_, last_):
        return (last_, first_) if h == 0 else (first_, last_)

    own = place(p, z, y, t)
    first = pltpu.make_async_copy(tok_in, tok.at[own, :, pl.ds(0, width)], load_sem.at[6])
    small = [pltpu.make_async_copy(ids_in, ids, load_sem.at[7]), pltpu.make_async_copy(rw_in, rw, load_sem.at[8])]
    for load in small:
        load.start()
    first.start()
    loads = [
        pltpu.make_async_copy(src, dst, load_sem.at[i])
        for i, (src, dst) in enumerate(
            ((sg_in, sg), (su_in, su), (wg_in.at[0], wg), (wu_in.at[0], wu), (wd_in.at[0], wd), (sd_in, sd))
        )
    ]
    for load in loads:
        load.start()

    for load in small:
        load.wait()
    lane = lax.broadcasted_iota(jnp.int32, (lay.extra, rows), 0)
    pieces = [jnp.zeros(lane.shape, F32) for _ in range(3)]
    for k in range(ids.shape[0]):
        for m in range(3):
            pieces[m] = pieces[m] + jnp.where(lane == ids[k : k + 1, :] + m * experts, rw[k : k + 1, :], 0.0)
    hi = [v.astype(BF16).astype(F32) for v in pieces]
    rest = [v - h for v, h in zip(pieces, hi)]
    mid = [v.astype(BF16).astype(F32) for v in rest]
    low = [v - h for v, h in zip(rest, mid)]
    mixed = (hi[0] + mid[1] + low[2]).astype(BF16)
    eye = (
        lax.broadcasted_iota(jnp.int32, (rows, rows), 0) == lax.broadcasted_iota(jnp.int32, (rows, rows), 1)
    ).astype(F32).astype(BF16)
    turned = lax.dot_general(eye, mixed, (((1,), (1,)), ((), ())), preferred_element_type=F32)
    tok[own, :, pl.ds(width, lay.extra)] = turned.astype(BF16)

    first.wait()
    pl.semaphore_wait(barrier, nt + ny + nz - 2)

    sent = []

    def send(src, dst, sem_send, sem_recv, dev):
        copy = pltpu.make_async_remote_copy(
            src_ref=src, dst_ref=dst, send_sem=sem_send, recv_sem=sem_recv, device_id=dev, device_id_type=MESH)
        copy.start()
        sent.append(copy)

    def got(dst, sem_recv):
        pltpu.make_async_remote_copy(
            src_ref=dst, dst_ref=dst, send_sem=red_send.at[0], recv_sem=sem_recv,
            device_id=partner, device_id_type=MESH).wait_recv()

    counter = [0]

    def send_block(h, idx, dev):
        view = tok.at[idx, :, wide[h]]
        send(view, view, tok_send.at[counter[0]], tok_recv.at[h, idx], dev)
        counter[0] += 1

    def arrive(h, idx):
        got(tok.at[idx, :, wide[h]], tok_recv.at[h, idx])

    def last_sends(h, idx):
        for v in last_peers[h]:
            send_block(h, idx, device(z, *yt(h, first_at[h], v)))

    def line_step(i):
        blk = place(p, seq[i], y, t)
        for h in slices:
            if i:
                arrive(h, blk)
            for v in first_peers[h]:
                send_block(h, blk, device(z, *yt(h, v, last_at[h])))
        for h in slices:
            last_sends(h, blk)
            send_block(h, blk, partner)

    def first_step(i):
        for h in slices:
            for f in first_peers[h]:
                blk = place(p, seq[i], *yt(h, f, last_at[h]))
                arrive(h, blk)
                last_sends(h, blk)
                send_block(h, blk, partner)

    def last_step(i):
        for h in slices:
            for f in [first_at[h]] + first_peers[h]:
                for v in last_peers[h]:
                    blk = place(p, seq[i], *yt(h, f, v))
                    arrive(h, blk)
                    send_block(h, blk, partner)

    def partner_wait(i):
        for y_ in range(ny):
            for t_ in range(nt):
                for h in slices:
                    arrive(h, place(other, seq[i], y_, t_))

    def hidden_tiles(x, w1, w2, scale, store):
        tile = tile_of(w1.shape[1], 512)
        for n in range(w1.shape[1] // tile):
            at = pl.ds(n * tile, tile)
            g = jnp.dot(x, w1[:, at], preferred_element_type=F32)
            u = jnp.dot(x, w2[:, at], preferred_element_type=F32)
            h = g / (1.0 + jnp.exp(-g)) * u
            if scale is not None:
                h = h * scale
            store[:, at] = h.astype(BF16)

    group = [place(q, z, y, t_) for q in range(2) for t_ in range(nt)]

    def shared_up(_):
        loads[0].wait()
        loads[1].wait()
        x = jnp.concatenate([tok[idx, :, pl.ds(0, width)] for idx in group], axis=0)
        hidden_tiles(x, sg, su, None, hs)

    mine = e_idx * 2 + p

    def up(i):
        if i == 0:
            loads[2].wait()
            loads[3].wait()
        at = pl.ds(seq[i] * lay.plane, lay.plane)
        extra = tok[at, :, pl.ds(width, lay.extra)].reshape(lay.plane * rows, lay.extra)
        l2 = lax.broadcasted_iota(jnp.int32, extra.shape, 1)
        pick = (l2 == mine) | (l2 == mine + experts) | (l2 == mine + 2 * experts)
        scale = jnp.sum(jnp.where(pick, extra.astype(F32), 0.0), axis=1, keepdims=True)
        hidden_tiles(tok[at, :, pl.ds(0, width)].reshape(lay.plane * rows, width), wg, wu, scale, hid)

    def down(i):
        if i == 0:
            loads[4].wait()
            loads[5].wait()
        zi = seq[i]
        for h in slices:
            v = jnp.dot(hid[...], wd[:, cols[h]], preferred_element_type=F32)
            part[pl.ds(zi * lay.plane, lay.plane), :, cols[h]] = v.astype(BF16).reshape(lay.plane, rows, lay.cols[h][1])
            if i == 0:
                v = jnp.dot(hs[...], sd[:, cols[h]], preferred_element_type=F32)
                for j, idx in enumerate(group):
                    part[idx, :, cols[h]] = (part[idx, :, cols[h]].astype(F32) + v[j * rows : (j + 1) * rows]).astype(BF16)
            send_sum(
                part.at[pl.ds(place(other, zi, 0, 0), chips), :, cols[h]],
                recvp.at[pl.ds(zi * chips, chips), :, cols[h]], pair_recv.at[h, zi], partner)

    rcount = [0]

    def send_sum(src, dst, sem_recv, dev):
        send(src, dst, red_send.at[rcount[0]], sem_recv, dev)
        rcount[0] += 1

    recvb, recva = (recvb0, recvb1), (recva0, recva1)

    def buf_b(h, d, z_, f):
        at = (d * nz + z_) * lay.first[h] + f
        return recvb[h].at[at], b_recv.at[h, at]

    def buf_a(h, d, z_):
        at = d * nz + z_
        return recva[h].at[at], a_recv.at[h, at]

    def buf_z(h, d):
        return recvz.at[d, :, cols[h]], z_recv.at[h, d]

    def add_into(h, idx, others):
        v = part[idx, :, cols[h]].astype(F32)
        for ref in others:
            v = v + ref[...].astype(F32)
        part[idx, :, cols[h]] = v.astype(BF16)

    def mine_of(z_, y_, t_, h):
        return recvp.at[(z_ * ny + y_) * nt + t_, :, cols[h]]

    def sums_last(i):
        z_ = seq[i]
        for h in slices:
            got(recvp.at[pl.ds(z_ * chips, chips), :, cols[h]], pair_recv.at[h, z_])
            for f in first_peers[h] + [first_at[h]]:
                for d, v in enumerate(last_peers[h]):
                    y_, t_ = yt(h, f, v)
                    idx = place(p, z_, y_, t_)
                    add_into(h, idx, [mine_of(z_, y_, t_, h)])
                    ref, sem = buf_b(h, d, z_, f)
                    send_sum(part.at[idx, :, cols[h]], ref, sem, device(z, *yt(h, first_at[h], v)))

    def collect_last(h, z_, f):
        y_, t_ = yt(h, f, last_at[h])
        refs = [mine_of(z_, y_, t_, h)]
        for d in range(lay.last[h] - 1):
            ref, sem = buf_b(h, d, z_, f)
            got(ref, sem)
            refs.append(ref)
        return place(p, z_, y_, t_), refs

    def sums_first(i):
        z_ = seq[i]
        for h in slices:
            for d, f in enumerate(first_peers[h]):
                idx, refs = collect_last(h, z_, f)
                add_into(h, idx, refs)
                ref, sem = buf_a(h, d, z_)
                send_sum(part.at[idx, :, cols[h]], ref, sem, device(z, *yt(h, f, last_at[h])))

    def sums_line(i):
        z_ = seq[i]
        for h in slices:
            idx, refs = collect_last(h, z_, first_at[h])
            for d in range(lay.first[h] - 1):
                ref, sem = buf_a(h, d, z_)
                got(ref, sem)
                refs.append(ref)
            add_into(h, idx, refs)
            if i:
                ref, sem = buf_z(h, (z_ - z + nz) % nz - 1)
                send_sum(part.at[idx, :, cols[h]], ref, sem, device(z_, y, t))

    line_order = [i for i in range(1, nz)]
    for i in line_order:
        for h in slices:
            send_block(h, own, device(seq[i], y, t))
    line_step(0)
    steps = {
        "A1": line_step, "A2": first_step, "A3": last_step, "W": partner_wait, "S": shared_up, "U": up, "D": down,
        "L": sums_last, "F": sums_first, "Z": sums_line,
    }
    for name, i in schedule(nz):
        steps[name](i)

    for h in slices:
        v = part[own, :, cols[h]].astype(F32)
        for d in range(nz - 1):
            ref, sem = buf_z(h, d)
            got(ref, sem)
            v = v + ref[...].astype(F32)
        out[:, cols[h]] = v.astype(BF16)
    for copy in sent:
        copy.wait_send()


def per_device(lay, experts, tokens, ids, rw, wg, wu, wd, sg, su, sd):
    rows, width = tokens.shape
    nz, ny, nt = lay.nz, lay.ny, lay.nt
    hidden, shared = wg.shape[2], sg.shape[1]
    n = len(lay.cols)
    sends = n * (nz - 1 + nz * (nt - 1 + ny - 1 + 1) + nz * (nt - 1 + ny - 1 + nt * ny) + nz * 2 * nt * ny) + n * nz * nt * ny
    red = n * nz * (1 + 2 * nt * ny + nt + ny + 1)
    many_b = [max(1, (lay.last[h] - 1) * nz * lay.first[h]) for h in range(2)]
    many_a = [max(1, (lay.first[h] - 1) * nz) for h in range(2)]
    halves = [c[1] for c in lay.cols]
    vmem = pl.BlockSpec(memory_space=pltpu.VMEM)
    anyw = pl.BlockSpec(memory_space=pl.ANY)
    scratch = [
        pltpu.VMEM((lay.blocks, rows, width + lay.extra), BF16),
        pltpu.VMEM((lay.blocks, rows, width), BF16),
        pltpu.VMEM(ids.shape, jnp.int32),
        pltpu.VMEM(rw.shape, F32),
        pltpu.VMEM((lay.blocks // 2, rows, width), BF16),
        pltpu.VMEM((many_b[0], rows, halves[0]), BF16),
        pltpu.VMEM((many_b[1], rows, halves[1]), BF16),
        pltpu.VMEM((many_a[0], rows, halves[0]), BF16),
        pltpu.VMEM((many_a[1], rows, halves[1]), BF16),
        pltpu.VMEM((max(1, nz - 1), rows, width), BF16),
        pltpu.VMEM((lay.plane * rows, hidden), BF16),
        pltpu.VMEM((2 * nt * rows, shared), BF16),
        pltpu.VMEM(wg.shape[1:], BF16),
        pltpu.VMEM(wu.shape[1:], BF16),
        pltpu.VMEM(wd.shape[1:], BF16),
        pltpu.VMEM(sg.shape, BF16),
        pltpu.VMEM(su.shape, BF16),
        pltpu.VMEM(sd.shape, BF16),
        pltpu.SemaphoreType.DMA((9,)),
        pltpu.SemaphoreType.DMA((sends,)),
        pltpu.SemaphoreType.DMA((n, lay.blocks)),
        pltpu.SemaphoreType.DMA((red,)),
        pltpu.SemaphoreType.DMA((n, nz)),
        pltpu.SemaphoreType.DMA((2, max(many_b))),
        pltpu.SemaphoreType.DMA((2, max(many_a))),
        pltpu.SemaphoreType.DMA((n, max(1, nz - 1))),
    ]
    return pl.pallas_call(
        functools.partial(kernel, lay, experts),
        out_shape=jax.ShapeDtypeStruct((rows, width), BF16),
        in_specs=[anyw] * 9,
        out_specs=vmem,
        scratch_shapes=scratch,
        compiler_params=pltpu.CompilerParams(
            collective_id=0, has_side_effects=True, vmem_limit_bytes=67043328
        ),
    )(tokens, ids, rw, wg, wu, wd, sg, su, sd)


def solution(mesh):
    shape = dict(mesh.shape)

    def body(tokens, ids, rw, wg, wu, wd, sg, su, sd):
        experts = shape["expert"] * shape["pair"] * wg.shape[0]
        lay = Layout(shape["expert"], shape["tensor"], tokens.shape[0], tokens.shape[1], experts)
        return per_device(lay, experts, tokens, ids.T, rw.T, wg, wu, wd, sg, su, sd)

    in_specs = (
        P(("groups", "expert", "tensor", "pair"), None),
        P(("groups", "expert", "tensor", "pair"), None),
        P(("groups", "expert", "tensor", "pair"), None),
        P(("expert", "pair"), None, "tensor"),
        P(("expert", "pair"), None, "tensor"),
        P(("expert", "pair"), "tensor", None),
        P(None, ("tensor", "pair")),
        P(None, ("tensor", "pair")),
        P(("tensor", "pair"), None),
    )
    out_specs = P(("groups", "expert", "tensor", "pair"), None)
    return jax.shard_map(body, mesh=mesh, in_specs=in_specs, out_specs=out_specs, check_vma=False)
```

```python
import functools

import jax
import jax.numpy as jnp
from jax import lax
from jax.experimental import pallas as pl
from jax.experimental.pallas import tpu as pltpu
from jax.sharding import PartitionSpec as P

MESH = pl.DeviceIdType.MESH
F32 = jnp.float32
BF16 = jnp.bfloat16


def lanes_for(experts):
    return -(-3 * experts // 128) * 128


def tile_of(width, most):
    for tile in range(min(width, most), 0, -1):
        if width % tile == 0 and (tile % 128 == 0 or tile == width):
            return tile
    return width


class Layout:
    def __init__(self, n_expert, n_tensor, tok_rows, width, experts):
        self.nt = n_tensor
        self.ny = 2 if n_expert % 2 == 0 else 1
        self.nz = n_expert // self.ny
        self.chips = self.ny * self.nt
        self.plane = 2 * self.chips
        self.blocks = self.nz * self.plane
        self.rows, self.width, self.extra = tok_rows, width, lanes_for(experts)
        units, at, self.cols = width // 128, 0, []
        for h in range(SLICES):
            n = (units * (h + 1) // SLICES - units * h // SLICES) * 128
            if h == SLICES - 1:
                n = width - at
            self.cols.append((at, n))
            at += n
        self.wide = self.cols[:-1] + [(self.cols[-1][0], self.cols[-1][1] + self.extra)]
        self.first = [(self.nt, self.ny)[h % 2] for h in range(SLICES)]
        self.last = [(self.ny, self.nt)[h % 2] for h in range(SLICES)]

    def sequence(self, z):
        nz = self.nz
        m = jnp.minimum(z, nz - 1 - z)
        out = [z]
        for i in range(1, nz):
            near = z + (i + 1) // 2 if i % 2 else z - i // 2
            far = jnp.where(z <= nz - 1 - z, z + (i - m), z - (i - m))
            out.append(jnp.where(i <= 2 * m, near, far))
        return out


SLICES = 2


def schedule(nz):
    ops = [("A2", 0), ("A1", 1), ("A1", 2), ("A3", 0), ("A2", 1), ("W", 0), ("S", 0), ("U", 0)]
    done = set()
    for i in range(nz):
        ops += [("A1", i + 3), ("A2", i + 2)]
        if i + 2 < nz:
            ops += [("A3", i + 1), ("D", i), ("W", i + 1), ("U", i + 1)]
        elif i + 1 < nz:
            ops += [("L", i - 1), ("D", i)] + [("L", j) for j in range(i - 1)]
            ops += [("A3", i + 1), ("L", i), ("W", i + 1), ("U", i + 1)]
        else:
            ops += [("D", i)]
    for j in range(1, nz - 1):
        ops.append(("F", j))
    ops.append(("L", nz - 1))
    for j in range(1, nz - 1):
        ops.append(("Z", j))
    ops += [("F", 0), ("F", nz - 1), ("Z", nz - 1), ("Z", 0)]
    out = []
    for op in ops:
        if 0 <= op[1] < nz and op not in out:
            out.append(op)
    return out


def kernel(lay, experts, tok_in, ids_in, rw_in, wg_in, wu_in, wd_in, sg_in, su_in, sd_in, out,
           tok, part, ids, rw, recvp, recvb, recva, recvz, hid, hs, wg, wu, wd, sg, su, sd,
           load_sem, bulk_send, line_send, line_recv, first_recv, last_recv, swap_recv, pair_recv, b_recv, a_recv, z_recv):
    nz, ny, nt = lay.nz, lay.ny, lay.nt
    rows, width, chips = lay.rows, lay.width, lay.chips
    e_idx, t, p = lax.axis_index("expert"), lax.axis_index("tensor"), lax.axis_index("pair")
    z, y = e_idx // ny, e_idx % ny
    other = 1 - p
    seq = lay.sequence(z)

    def device(z_, y_, t_):
        return {"expert": z_ * ny + y_, "tensor": t_, "pair": p}

    partner = {"expert": e_idx, "tensor": t, "pair": other}
    t_peers = [(t + d) % nt for d in range(1, nt)]
    y_peers = [(y + d) % ny for d in range(1, ny)]

    barrier = pltpu.get_barrier_semaphore()

    def greet(dev):
        pl.semaphore_signal(barrier, inc=1, device_id=dev, device_id_type=MESH)

    for d in range(1, nz):
        greet(device((z + d) % nz, y, t))
    for t_ in t_peers:
        greet(device(z, y, t_))
    for y_ in y_peers:
        greet(device(z, y_, t))
    greet(partner)

    def place(q, z_, y_, t_):
        return ((z_ * 2 + q) * ny + y_) * nt + t_

    cols = [pl.ds(a, n) for a, n in lay.cols]
    wide = [pl.ds(a, n) for a, n in lay.wide]
    slices = range(len(cols))
    first_peers = [(t_peers, y_peers)[h % 2] for h in slices]
    last_peers = [(y_peers, t_peers)[h % 2] for h in slices]
    first_at = [(t, y)[h % 2] for h in slices]
    last_at = [(y, t)[h % 2] for h in slices]

    def yt(h, first_, last_):
        return (last_, first_) if h % 2 == 0 else (first_, last_)

    own = place(p, z, y, t)
    first = pltpu.make_async_copy(tok_in, tok.at[own, :, pl.ds(0, width)], load_sem.at[6])
    small = [pltpu.make_async_copy(ids_in, ids, load_sem.at[7]), pltpu.make_async_copy(rw_in, rw, load_sem.at[8])]
    for load in small:
        load.start()
    first.start()
    loads = [
        pltpu.make_async_copy(src, dst, load_sem.at[i])
        for i, (src, dst) in enumerate(
            ((sg_in, sg), (su_in, su), (wg_in.at[0], wg), (wu_in.at[0], wu), (wd_in.at[0], wd), (sd_in, sd))
        )
    ]
    for load in loads:
        load.start()

    for load in small:
        load.wait()
    lane = lax.broadcasted_iota(jnp.int32, (lay.extra, rows), 0)
    pieces = [jnp.zeros(lane.shape, F32) for _ in range(3)]
    for k in range(ids.shape[0]):
        for m in range(3):
            pieces[m] = pieces[m] + jnp.where(lane == ids[k : k + 1, :] + m * experts, rw[k : k + 1, :], 0.0)
    hi = [v.astype(BF16).astype(F32) for v in pieces]
    rest = [v - h for v, h in zip(pieces, hi)]
    mid = [v.astype(BF16).astype(F32) for v in rest]
    low = [v - h for v, h in zip(rest, mid)]
    mixed = (hi[0] + mid[1] + low[2]).astype(BF16)
    eye = (
        lax.broadcasted_iota(jnp.int32, (rows, rows), 0) == lax.broadcasted_iota(jnp.int32, (rows, rows), 1)
    ).astype(F32).astype(BF16)
    turned = lax.dot_general(eye, mixed, (((1,), (1,)), ((), ())), preferred_element_type=F32)
    tok[own, :, pl.ds(width, lay.extra)] = turned.astype(BF16)

    first.wait()
    pl.semaphore_wait(barrier, nt + ny + nz - 2)

    def remote(src, dst, sem_send, sem_recv, dev):
        return pltpu.make_async_remote_copy(
            src_ref=src, dst_ref=dst, send_sem=sem_send, recv_sem=sem_recv, device_id=dev, device_id_type=MESH)

    def got(view, sem_recv):
        remote(view, view, bulk_send.at[0, 0], sem_recv, partner).wait_recv()

    counts = {}

    def send(kind, h, src, dst, sem_recv, dev, blocks=1):
        remote(src, dst, bulk_send.at[kind, h], sem_recv, dev).start()
        counts[kind, h] = counts.get((kind, h), 0) + blocks

    def send_block(kind, h, idx, sem_recv, dev):
        view = tok.at[idx, :, wide[h]]
        send(kind, h, view, view, sem_recv, dev)

    line_sent = []

    def send_line(slot, idx, z_, target):
        ok = (target >= 0) & (target < nz)
        dev = device(target, y, t)

        def whole():
            remote(tok.at[idx], tok.at[idx], line_send.at[slot], line_recv.at[0, 0], dev).wait_send()

        def part_of(h):
            view = tok.at[idx, :, wide[h]]
            pl.when(ok)(remote(view, view, line_send.at[slot], line_recv.at[h, z_], dev).start)

        line_sent.append((ok, whole))
        return part_of

    def last_sends(h, idx, z_):
        for v in last_peers[h]:
            send_block(1, h, idx, last_recv.at[h, z_], device(z, *yt(h, first_at[h], v)))

    def swap(h, idx, z_):
        send_block(2, h, idx, swap_recv.at[z_], partner)

    def line_step(i):
        z_ = seq[i]
        blk = place(p, z_, y, t)
        if i == 0:
            onward = [send_line(0, blk, z_, z + 1), send_line(nz, blk, z_, z - 1)]
        else:
            onward = [send_line(i, blk, z_, jnp.where(z_ < z, z + 1, z - 1))]
        for h in slices:
            if i:
                got(tok.at[blk, :, wide[h]], line_recv.at[h, z_])
            for part_of in onward:
                part_of(h)
            for d, v in enumerate(first_peers[h]):
                send_block(0, h, blk, first_recv.at[h, d * nz + z_], device(z, *yt(h, v, last_at[h])))
        for h in slices:
            last_sends(h, blk, z_)
            swap(h, blk, z_)

    def first_step(i):
        z_ = seq[i]
        for h in slices:
            n = lay.first[h]
            for d in range(n - 1):
                f = (first_at[h] + n - 1 - d) % n
                blk = place(p, z_, *yt(h, f, last_at[h]))
                got(tok.at[blk, :, wide[h]], first_recv.at[h, d * nz + z_])
                last_sends(h, blk, z_)
                swap(h, blk, z_)

    def last_step(i):
        z_ = seq[i]
        for h in slices:
            n = lay.first[h] * (lay.last[h] - 1)
            if n:
                got(tok.at[pl.ds(0, n), :, wide[h]], last_recv.at[h, z_])
            for f in [first_at[h]] + first_peers[h]:
                for v in last_peers[h]:
                    swap(h, place(p, z_, *yt(h, f, v)), z_)

    def partner_wait(i):
        got(tok.at[pl.ds(place(other, seq[i], 0, 0), chips)], swap_recv.at[seq[i]])

    def hidden_tiles(x, w1, w2, scale, store):
        tile = tile_of(w1.shape[1], 512)
        for n in range(w1.shape[1] // tile):
            at = pl.ds(n * tile, tile)
            g = jnp.dot(x, w1[:, at], preferred_element_type=F32)
            u = jnp.dot(x, w2[:, at], preferred_element_type=F32)
            h = g / (1.0 + jnp.exp(-g)) * u
            if scale is not None:
                h = h * scale
            store[:, at] = h.astype(BF16)

    group = [place(q, z, y, t_) for q in range(2) for t_ in range(nt)]

    def shared_up(_):
        loads[0].wait()
        loads[1].wait()
        x = jnp.concatenate([tok[idx, :, pl.ds(0, width)] for idx in group], axis=0)
        hidden_tiles(x, sg, su, None, hs)

    mine = e_idx * 2 + p

    def up(i):
        if i == 0:
            loads[2].wait()
            loads[3].wait()
        at = pl.ds(seq[i] * lay.plane, lay.plane)
        extra = tok[at, :, pl.ds(width, lay.extra)].reshape(lay.plane * rows, lay.extra)
        l2 = lax.broadcasted_iota(jnp.int32, extra.shape, 1)
        pick = (l2 == mine) | (l2 == mine + experts) | (l2 == mine + 2 * experts)
        scale = jnp.sum(jnp.where(pick, extra.astype(F32), 0.0), axis=1, keepdims=True)
        hidden_tiles(tok[at, :, pl.ds(0, width)].reshape(lay.plane * rows, width), wg, wu, scale, hid)

    def down(i):
        if i == 0:
            loads[4].wait()
            loads[5].wait()
        z_ = seq[i]
        for h in slices:
            v = jnp.dot(hid[...], wd[:, cols[h]], preferred_element_type=F32)
            part[pl.ds(z_ * lay.plane, lay.plane), :, cols[h]] = v.astype(BF16).reshape(lay.plane, rows, lay.cols[h][1])
            if i == 0:
                v = jnp.dot(hs[...], sd[:, cols[h]], preferred_element_type=F32)
                for j, idx in enumerate(group):
                    part[idx, :, cols[h]] = (part[idx, :, cols[h]].astype(F32) + v[j * rows : (j + 1) * rows]).astype(BF16)
            send(3, h, part.at[pl.ds(place(other, z_, 0, 0), chips), :, cols[h]],
                 recvp.at[pl.ds(z_ * chips, chips), :, cols[h]], pair_recv.at[h, z_], partner, chips)

    def buf_b(h, d, z_, f):
        return recvb.at[(d * nz + z_) * lay.first[h] + f, :, cols[h]]

    def buf_a(h, d, z_):
        return recva.at[d * nz + z_, :, cols[h]]

    def add_into(h, idx, others):
        v = part[idx, :, cols[h]].astype(F32)
        for ref in others:
            v = v + ref[...].astype(F32)
        part[idx, :, cols[h]] = v.astype(BF16)

    def mine_of(z_, y_, t_, h):
        return recvp.at[(z_ * ny + y_) * nt + t_, :, cols[h]]

    def sums_last(i):
        z_ = seq[i]
        for h in slices:
            got(recvp.at[pl.ds(z_ * chips, chips), :, cols[h]], pair_recv.at[h, z_])
            for k, f in enumerate(first_peers[h] + [first_at[h]]):
                here = int(k == lay.first[h] - 1)
                for d, v in enumerate(last_peers[h]):
                    y_, t_ = yt(h, f, v)
                    idx = place(p, z_, y_, t_)
                    add_into(h, idx, [mine_of(z_, y_, t_, h)])
                    send(4, h, part.at[idx, :, cols[h]], buf_b(h, d, z_, f), b_recv.at[h, here * nz + z_],
                         device(z, *yt(h, first_at[h], v)))

    def collect_last(h, z_, f):
        y_, t_ = yt(h, f, last_at[h])
        return place(p, z_, y_, t_), [mine_of(z_, y_, t_, h)] + [buf_b(h, d, z_, f) for d in range(lay.last[h] - 1)]

    def sums_first(i):
        z_ = seq[i]
        for h in slices:
            n = (lay.first[h] - 1) * (lay.last[h] - 1)
            if n:
                got(recvb.at[pl.ds(0, n), :, cols[h]], b_recv.at[h, z_])
            for d, f in enumerate(first_peers[h]):
                idx, refs = collect_last(h, z_, f)
                add_into(h, idx, refs)
                send(5, h, part.at[idx, :, cols[h]], buf_a(h, d, z_), a_recv.at[h, z_], device(z, *yt(h, f, last_at[h])))

    def sums_line(i):
        z_ = seq[i]
        for h in slices:
            if lay.last[h] > 1:
                got(recvb.at[pl.ds(0, lay.last[h] - 1), :, cols[h]], b_recv.at[h, nz + z_])
            if lay.first[h] > 1:
                got(recva.at[pl.ds(0, lay.first[h] - 1), :, cols[h]], a_recv.at[h, z_])
            idx, refs = collect_last(h, z_, first_at[h])
            add_into(h, idx, refs + [buf_a(h, d, z_) for d in range(lay.first[h] - 1)])
            if i:
                slot = (z_ - z + nz) % nz - 1
                send(6, h, part.at[idx, :, cols[h]], recvz.at[slot, :, cols[h]], z_recv.at[h], device(z_, y, t))

    line_step(0)
    steps = {
        "A1": line_step, "A2": first_step, "A3": last_step, "W": partner_wait, "S": shared_up, "U": up, "D": down,
        "L": sums_last, "F": sums_first, "Z": sums_line,
    }
    for name, i in schedule(nz):
        steps[name](i)

    for h in slices:
        if nz > 1:
            got(recvz.at[pl.ds(0, nz - 1), :, cols[h]], z_recv.at[h])
        v = part[own, :, cols[h]].astype(F32)
        for d in range(nz - 1):
            v = v + recvz[d, :, cols[h]].astype(F32)
        out[:, cols[h]] = v.astype(BF16)
    for ok, whole in line_sent:
        pl.when(ok)(whole)
    for (kind, h), n in counts.items():
        view = (tok if kind < 3 else part).at[pl.ds(0, n), :, (wide if kind < 3 else cols)[h]]
        remote(view, view, bulk_send.at[kind, h], z_recv.at[h], partner).wait_send()


def per_device(lay, experts, tokens, ids, rw, wg, wu, wd, sg, su, sd):
    rows, width = tokens.shape
    nz, ny, nt = lay.nz, lay.ny, lay.nt
    hidden, shared = wg.shape[2], sg.shape[1]
    n, most = len(lay.cols), max(nt, ny)
    many_b = max(1, max((lay.last[h] - 1) * lay.first[h] for h in range(n)) * nz)
    many_a = max(1, (most - 1) * nz)
    vmem = pl.BlockSpec(memory_space=pltpu.VMEM)
    anyw = pl.BlockSpec(memory_space=pl.ANY)
    dma = pltpu.SemaphoreType.DMA
    scratch = [
        pltpu.VMEM((lay.blocks, rows, width + lay.extra), BF16),
        pltpu.VMEM((lay.blocks, rows, width), BF16),
        pltpu.VMEM(ids.shape, jnp.int32),
        pltpu.VMEM(rw.shape, F32),
        pltpu.VMEM((lay.blocks // 2, rows, width), BF16),
        pltpu.VMEM((many_b, rows, width), BF16),
        pltpu.VMEM((many_a, rows, width), BF16),
        pltpu.VMEM((max(1, nz - 1), rows, width), BF16),
        pltpu.VMEM((lay.plane * rows, hidden), BF16),
        pltpu.VMEM((2 * nt * rows, shared), BF16),
        pltpu.VMEM(wg.shape[1:], BF16),
        pltpu.VMEM(wu.shape[1:], BF16),
        pltpu.VMEM(wd.shape[1:], BF16),
        pltpu.VMEM(sg.shape, BF16),
        pltpu.VMEM(su.shape, BF16),
        pltpu.VMEM(sd.shape, BF16),
        dma((9,)),
        dma((7, n)),
        dma((nz + 1,)),
        dma((n, nz)),
        dma((n, nz * max(1, most - 1))),
        dma((n, nz)),
        dma((nz,)),
        dma((n, nz)),
        dma((n, 2 * nz)),
        dma((n, nz)),
        dma((n,)),
    ]
    return pl.pallas_call(
        functools.partial(kernel, lay, experts),
        out_shape=jax.ShapeDtypeStruct((rows, width), BF16),
        in_specs=[anyw] * 9,
        out_specs=vmem,
        scratch_shapes=scratch,
        compiler_params=pltpu.CompilerParams(
            collective_id=0, has_side_effects=True, vmem_limit_bytes=67043328
        ),
    )(tokens, ids, rw, wg, wu, wd, sg, su, sd)


def solution(mesh):
    shape = dict(mesh.shape)

    def body(tokens, ids, rw, wg, wu, wd, sg, su, sd):
        experts = shape["expert"] * shape["pair"] * wg.shape[0]
        lay = Layout(shape["expert"], shape["tensor"], tokens.shape[0], tokens.shape[1], experts)
        return per_device(lay, experts, tokens, ids.T, rw.T, wg, wu, wd, sg, su, sd)

    in_specs = (
        P(("groups", "expert", "tensor", "pair"), None),
        P(("groups", "expert", "tensor", "pair"), None),
        P(("groups", "expert", "tensor", "pair"), None),
        P(("expert", "pair"), None, "tensor"),
        P(("expert", "pair"), None, "tensor"),
        P(("expert", "pair"), "tensor", None),
        P(None, ("tensor", "pair")),
        P(None, ("tensor", "pair")),
        P(("tensor", "pair"), None),
    )
    out_specs = P(("groups", "expert", "tensor", "pair"), None)
    return jax.shard_map(body, mesh=mesh, in_specs=in_specs, out_specs=out_specs, check_vma=False)
```

```python
import functools

import jax
import jax.numpy as jnp
from jax import lax
from jax.experimental import pallas as pl
from jax.experimental.pallas import tpu as pltpu
from jax.sharding import PartitionSpec as P

MESH = pl.DeviceIdType.MESH
F32 = jnp.float32
BF16 = jnp.bfloat16


def lanes_for(experts):
    return -(-3 * experts // 128) * 128


def tile_of(width, most):
    for tile in range(min(width, most), 0, -1):
        if width % tile == 0 and (tile % 128 == 0 or tile == width):
            return tile
    return width


class Layout:
    def __init__(self, n_expert, n_tensor, tok_rows, width, experts):
        self.nt = n_tensor
        self.ny = 2 if n_expert % 2 == 0 else 1
        self.nz = n_expert // self.ny
        self.chips = self.ny * self.nt
        self.plane = 2 * self.chips
        self.blocks = self.nz * self.plane
        self.rows, self.width, self.extra = tok_rows, width, lanes_for(experts)
        units, at, self.cols = width // 128, 0, []
        for h in range(SLICES):
            n = (units * (h + 1) // SLICES - units * h // SLICES) * 128
            if h == SLICES - 1:
                n = width - at
            self.cols.append((at, n))
            at += n
        self.wide = self.cols[:-1] + [(self.cols[-1][0], self.cols[-1][1] + self.extra)]
        self.first = [(self.nt, self.ny)[h % 2] for h in range(SLICES)]
        self.last = [(self.ny, self.nt)[h % 2] for h in range(SLICES)]

    def sequences(self, z):
        nz = self.nz
        m = jnp.minimum(z, nz - 1 - z)
        side = jnp.where(z <= nz - 1 - z, 1, -1)
        hops, taken = [z], [z]
        for i in range(1, nz):
            near = z + side * ((i + 1) // 2) if i % 2 else z - side * (i // 2)
            hops.append(jnp.where(i <= 2 * m, near, z + side * (i - m)))
            moved = z + side * (i + 1 - m) if i < nz - 1 else z - side * m
            taken.append(jnp.where(m == 0, z + side * i, jnp.where(i < 2 * m, near, moved)))
        return hops, taken


SLICES = 2


def schedule(nz):
    ops = ["A2 0", "R 1", "A1m 1", "A1e 1", "R 2", "A1e 2", "R 3", "A1m 2", "A3 0", "A2 1"]
    ops += [f"R {i}" for i in range(4, nz)]
    ops += ["A1m 3", "W 0", "S 0", "U 0"]
    for i in range(nz):
        ops += [f"A1m {i + 4}", f"A1e {i + 3}", f"A2 {i + 2}", f"A3 {i + 1}", f"L {i - 1}" if i > 1 else "", f"D {i}"]
        ops += [f"W {i + 1}", f"A2 {i + 3}", f"U {i + 1}", "L 0"]
    ops += ["F 1", f"L {nz - 1}"]
    for j in range(2, nz - 1):
        ops += [f"F {j}", f"Z {j - 1}"]
    ops += [f"F {nz - 1}", "F 0", f"Z {nz - 2}", f"Z {nz - 1}", "Z 0"]
    return tidy(ops, nz)


def tidy(ops, nz):
    out = []
    for op in ops:
        if op and op not in out and int(op.split()[1]) < nz:
            out.append(op)
    return [(op.split()[0], int(op.split()[1])) for op in out]


def kernel(lay, experts, tok_in, ids_in, rw_in, wg_in, wu_in, wd_in, sg_in, su_in, sd_in, out,
           tok, part, ids, rw, recvp, recvb, recva, recvz, hid, hs, wg, wu, wd, sg, su, sd,
           load_sem, bulk_send, line_send, line_recv, first_recv, last_recv, swap_recv, pair_recv, b_recv, a_recv, z_recv):
    nz, ny, nt = lay.nz, lay.ny, lay.nt
    rows, width, chips = lay.rows, lay.width, lay.chips
    e_idx, t, p = lax.axis_index("expert"), lax.axis_index("tensor"), lax.axis_index("pair")
    z, y = e_idx // ny, e_idx % ny
    other = 1 - p
    hops, seq = lay.sequences(z)

    def device(z_, y_, t_):
        return {"expert": z_ * ny + y_, "tensor": t_, "pair": p}

    partner = {"expert": e_idx, "tensor": t, "pair": other}
    t_peers = [(t + d) % nt for d in range(1, nt)]
    y_peers = [(y + d) % ny for d in range(1, ny)]

    barrier = pltpu.get_barrier_semaphore()

    def greet(dev):
        pl.semaphore_signal(barrier, inc=1, device_id=dev, device_id_type=MESH)

    for d in range(1, nz):
        greet(device((z + d) % nz, y, t))
    for t_ in t_peers:
        greet(device(z, y, t_))
    for y_ in y_peers:
        greet(device(z, y_, t))
    greet(partner)

    def place(q, z_, y_, t_):
        return ((z_ * 2 + q) * ny + y_) * nt + t_

    cols = [pl.ds(a, n) for a, n in lay.cols]
    wide = [pl.ds(a, n) for a, n in lay.wide]
    slices = range(len(cols))
    first_peers = [(t_peers, y_peers)[h % 2] for h in slices]
    last_peers = [(y_peers, t_peers)[h % 2] for h in slices]
    first_at = [(t, y)[h % 2] for h in slices]
    last_at = [(y, t)[h % 2] for h in slices]

    def yt(h, first_, last_):
        return (last_, first_) if h % 2 == 0 else (first_, last_)

    own = place(p, z, y, t)
    first = pltpu.make_async_copy(tok_in, tok.at[own, :, pl.ds(0, width)], load_sem.at[6])
    small = [pltpu.make_async_copy(ids_in, ids, load_sem.at[7]), pltpu.make_async_copy(rw_in, rw, load_sem.at[8])]
    for load in small:
        load.start()
    first.start()
    loads = [
        pltpu.make_async_copy(src, dst, load_sem.at[i])
        for i, (src, dst) in enumerate(
            ((sg_in, sg), (su_in, su), (wg_in.at[0], wg), (wu_in.at[0], wu), (wd_in.at[0], wd), (sd_in, sd))
        )
    ]
    for load in loads:
        load.start()

    for load in small:
        load.wait()
    lane = lax.broadcasted_iota(jnp.int32, (lay.extra, rows), 0)
    pieces = [jnp.zeros(lane.shape, F32) for _ in range(3)]
    for k in range(ids.shape[0]):
        for m in range(3):
            pieces[m] = pieces[m] + jnp.where(lane == ids[k : k + 1, :] + m * experts, rw[k : k + 1, :], 0.0)
    hi = [v.astype(BF16).astype(F32) for v in pieces]
    rest = [v - h for v, h in zip(pieces, hi)]
    mid = [v.astype(BF16).astype(F32) for v in rest]
    low = [v - h for v, h in zip(rest, mid)]
    mixed = (hi[0] + mid[1] + low[2]).astype(BF16)
    eye = (
        lax.broadcasted_iota(jnp.int32, (rows, rows), 0) == lax.broadcasted_iota(jnp.int32, (rows, rows), 1)
    ).astype(F32).astype(BF16)
    turned = lax.dot_general(eye, mixed, (((1,), (1,)), ((), ())), preferred_element_type=F32)
    tok[own, :, pl.ds(width, lay.extra)] = turned.astype(BF16)

    first.wait()
    pl.semaphore_wait(barrier, nt + ny + nz - 2)

    def remote(src, dst, sem_send, sem_recv, dev):
        return pltpu.make_async_remote_copy(
            src_ref=src, dst_ref=dst, send_sem=sem_send, recv_sem=sem_recv, device_id=dev, device_id_type=MESH)

    def got(view, sem_recv):
        remote(view, view, bulk_send.at[0, 0], sem_recv, partner).wait_recv()

    counts = {}

    def send(kind, h, src, dst, sem_recv, dev, blocks=1):
        remote(src, dst, bulk_send.at[kind, h], sem_recv, dev).start()
        counts[kind, h] = counts.get((kind, h), 0) + blocks

    def send_block(kind, h, idx, sem_recv, dev):
        view = tok.at[idx, :, wide[h]]
        send(kind, h, view, view, sem_recv, dev)

    line_sent = []

    def send_line(slot, idx, z_, target):
        ok = (target >= 0) & (target < nz)
        dev = device(target, y, t)

        def whole():
            remote(tok.at[idx], tok.at[idx], line_send.at[slot], line_recv.at[0, 0], dev).wait_send()

        def part_of(h):
            view = tok.at[idx, :, wide[h]]
            copy = remote(view, view, line_send.at[slot], line_recv.at[h, z_], dev)
            if slot in (0, nz):
                pl.when(ok)(copy.start)
            else:
                copy.start()

        line_sent.append((ok, whole))
        return part_of

    def last_sends(h, idx, z_):
        for v in last_peers[h]:
            send_block(1, h, idx, last_recv.at[h, z_], device(z, *yt(h, first_at[h], v)))

    def swap(h, idx, z_):
        send_block(2, h, idx, swap_recv.at[z_], partner)

    def inner(z_):
        target = jnp.where(z_ < z, z + 1, z - 1)
        return target, (target >= 0) & (target < nz)

    def take(i):
        blk = place(p, seq[i], y, t)
        for h in slices:
            got(tok.at[blk, :, wide[h]], line_recv.at[h, seq[i]])

    def relay_step(i):
        z_ = hops[i]
        target, ok = inner(z_)
        blk = place(p, z_, y, t)
        part_of = send_line(i, blk, z_, target)

        def go():
            for h in slices:
                got(tok.at[blk, :, wide[h]], line_recv.at[h, z_])
                part_of(h)

        pl.when(ok)(go)

    def spread(i):
        z_ = seq[i]
        blk = place(p, z_, y, t)
        for h in slices:
            for d, v in enumerate(first_peers[h]):
                send_block(0, h, blk, first_recv.at[h, d * nz + z_], device(z, *yt(h, v, last_at[h])))
        for h in slices:
            last_sends(h, blk, z_)
            swap(h, blk, z_)

    def inner_step(i):
        pl.when(inner(seq[i])[1])(lambda: spread(i))

    def outer_step(i):
        kept = dict(counts)

        def go():
            take(i)
            spread(i)

        pl.when(jnp.logical_not(inner(seq[i])[1]))(go)
        counts.clear()
        counts.update(kept)

    def start_step():
        up, down_ = send_line(0, own, z, z + 1), send_line(nz, own, z, z - 1)
        for h in slices:
            up(h)
            down_(h)
        spread(0)

    def first_step(i):
        z_ = seq[i]
        for h in slices:
            n = lay.first[h]
            for d in range(n - 1):
                f = (first_at[h] + n - 1 - d) % n
                blk = place(p, z_, *yt(h, f, last_at[h]))
                got(tok.at[blk, :, wide[h]], first_recv.at[h, d * nz + z_])
                last_sends(h, blk, z_)
                swap(h, blk, z_)

    def last_step(i):
        z_ = seq[i]
        for h in slices:
            n = lay.first[h] * (lay.last[h] - 1)
            if n:
                got(tok.at[pl.ds(0, n), :, wide[h]], last_recv.at[h, z_])
            for f in [first_at[h]] + first_peers[h]:
                for v in last_peers[h]:
                    swap(h, place(p, z_, *yt(h, f, v)), z_)

    def partner_wait(i):
        got(tok.at[pl.ds(place(other, seq[i], 0, 0), chips)], swap_recv.at[seq[i]])

    def hidden_tiles(x, w1, w2, scale, store):
        tile = tile_of(w1.shape[1], 512)
        for n in range(w1.shape[1] // tile):
            at = pl.ds(n * tile, tile)
            g = jnp.dot(x, w1[:, at], preferred_element_type=F32)
            u = jnp.dot(x, w2[:, at], preferred_element_type=F32)
            h = g / (1.0 + jnp.exp(-g)) * u
            if scale is not None:
                h = h * scale
            store[:, at] = h.astype(BF16)

    group = [place(q, z, y, t_) for q in range(2) for t_ in range(nt)]

    def shared_up(_):
        loads[0].wait()
        loads[1].wait()
        x = jnp.concatenate([tok[idx, :, pl.ds(0, width)] for idx in group], axis=0)
        hidden_tiles(x, sg, su, None, hs)

    mine = e_idx * 2 + p

    def up(i):
        if i == 0:
            loads[2].wait()
            loads[3].wait()
        at = pl.ds(seq[i] * lay.plane, lay.plane)
        extra = tok[at, :, pl.ds(width, lay.extra)].reshape(lay.plane * rows, lay.extra)
        l2 = lax.broadcasted_iota(jnp.int32, extra.shape, 1)
        pick = (l2 == mine) | (l2 == mine + experts) | (l2 == mine + 2 * experts)
        scale = jnp.sum(jnp.where(pick, extra.astype(F32), 0.0), axis=1, keepdims=True)
        hidden_tiles(tok[at, :, pl.ds(0, width)].reshape(lay.plane * rows, width), wg, wu, scale, hid)

    def down(i):
        if i == 0:
            loads[4].wait()
            loads[5].wait()
        z_ = seq[i]
        for h in slices:
            v = jnp.dot(hid[...], wd[:, cols[h]], preferred_element_type=F32)
            part[pl.ds(z_ * lay.plane, lay.plane), :, cols[h]] = v.astype(BF16).reshape(lay.plane, rows, lay.cols[h][1])
            if i == 0:
                v = jnp.dot(hs[...], sd[:, cols[h]], preferred_element_type=F32)
                for j, idx in enumerate(group):
                    part[idx, :, cols[h]] = (part[idx, :, cols[h]].astype(F32) + v[j * rows : (j + 1) * rows]).astype(BF16)
            send(3, h, part.at[pl.ds(place(other, z_, 0, 0), chips), :, cols[h]],
                 recvp.at[pl.ds(z_ * chips, chips), :, cols[h]], pair_recv.at[h, z_], partner, chips)

    def buf_b(h, d, z_, f):
        return recvb.at[(d * nz + z_) * lay.first[h] + f, :, cols[h]]

    def buf_a(h, d, z_):
        return recva.at[d * nz + z_, :, cols[h]]

    def add_into(h, idx, others):
        v = part[idx, :, cols[h]].astype(F32)
        for ref in others:
            v = v + ref[...].astype(F32)
        part[idx, :, cols[h]] = v.astype(BF16)

    def mine_of(z_, y_, t_, h):
        return recvp.at[(z_ * ny + y_) * nt + t_, :, cols[h]]

    def sums_last(i):
        z_ = seq[i]
        for h in slices:
            got(recvp.at[pl.ds(z_ * chips, chips), :, cols[h]], pair_recv.at[h, z_])
            for k, f in enumerate(first_peers[h] + [first_at[h]]):
                here = int(k == lay.first[h] - 1)
                for d, v in enumerate(last_peers[h]):
                    y_, t_ = yt(h, f, v)
                    idx = place(p, z_, y_, t_)
                    add_into(h, idx, [mine_of(z_, y_, t_, h)])
                    send(4, h, part.at[idx, :, cols[h]], buf_b(h, d, z_, f), b_recv.at[h, here * nz + z_],
                         device(z, *yt(h, first_at[h], v)))

    def collect_last(h, z_, f):
        y_, t_ = yt(h, f, last_at[h])
        return place(p, z_, y_, t_), [mine_of(z_, y_, t_, h)] + [buf_b(h, d, z_, f) for d in range(lay.last[h] - 1)]

    def sums_first(i):
        z_ = seq[i]
        for h in slices:
            n = (lay.first[h] - 1) * (lay.last[h] - 1)
            if n:
                got(recvb.at[pl.ds(0, n), :, cols[h]], b_recv.at[h, z_])
            for d, f in enumerate(first_peers[h]):
                idx, refs = collect_last(h, z_, f)
                add_into(h, idx, refs)
                send(5, h, part.at[idx, :, cols[h]], buf_a(h, d, z_), a_recv.at[h, z_], device(z, *yt(h, f, last_at[h])))

    def sums_line(i):
        z_ = seq[i]
        for h in slices:
            if lay.last[h] > 1:
                got(recvb.at[pl.ds(0, lay.last[h] - 1), :, cols[h]], b_recv.at[h, nz + z_])
            if lay.first[h] > 1:
                got(recva.at[pl.ds(0, lay.first[h] - 1), :, cols[h]], a_recv.at[h, z_])
            idx, refs = collect_last(h, z_, first_at[h])
            add_into(h, idx, refs + [buf_a(h, d, z_) for d in range(lay.first[h] - 1)])
            if i:
                slot = (z_ - z + nz) % nz - 1
                send(6, h, part.at[idx, :, cols[h]], recvz.at[slot, :, cols[h]], z_recv.at[h], device(z_, y, t))

    start_step()
    steps = {
        "R": relay_step, "A1m": inner_step, "A1e": outer_step, "A2": first_step, "A3": last_step, "W": partner_wait, "S": shared_up, "U": up, "D": down,
        "L": sums_last, "F": sums_first, "Z": sums_line,
    }
    for name, i in schedule(nz):
        steps[name](i)

    for h in slices:
        if nz > 1:
            got(recvz.at[pl.ds(0, nz - 1), :, cols[h]], z_recv.at[h])
        v = part[own, :, cols[h]].astype(F32)
        for d in range(nz - 1):
            v = v + recvz[d, :, cols[h]].astype(F32)
        out[:, cols[h]] = v.astype(BF16)
    for ok, whole in line_sent:
        pl.when(ok)(whole)
    for (kind, h), n in counts.items():
        view = (tok if kind < 3 else part).at[pl.ds(0, n), :, (wide if kind < 3 else cols)[h]]
        remote(view, view, bulk_send.at[kind, h], z_recv.at[h], partner).wait_send()


def per_device(lay, experts, tokens, ids, rw, wg, wu, wd, sg, su, sd):
    rows, width = tokens.shape
    nz, ny, nt = lay.nz, lay.ny, lay.nt
    hidden, shared = wg.shape[2], sg.shape[1]
    n, most = len(lay.cols), max(nt, ny)
    many_b = max(1, max((lay.last[h] - 1) * lay.first[h] for h in range(n)) * nz)
    many_a = max(1, (most - 1) * nz)
    vmem = pl.BlockSpec(memory_space=pltpu.VMEM)
    anyw = pl.BlockSpec(memory_space=pl.ANY)
    dma = pltpu.SemaphoreType.DMA
    scratch = [
        pltpu.VMEM((lay.blocks, rows, width + lay.extra), BF16),
        pltpu.VMEM((lay.blocks, rows, width), BF16),
        pltpu.VMEM(ids.shape, jnp.int32),
        pltpu.VMEM(rw.shape, F32),
        pltpu.VMEM((lay.blocks // 2, rows, width), BF16),
        pltpu.VMEM((many_b, rows, width), BF16),
        pltpu.VMEM((many_a, rows, width), BF16),
        pltpu.VMEM((max(1, nz - 1), rows, width), BF16),
        pltpu.VMEM((lay.plane * rows, hidden), BF16),
        pltpu.VMEM((2 * nt * rows, shared), BF16),
        pltpu.VMEM(wg.shape[1:], BF16),
        pltpu.VMEM(wu.shape[1:], BF16),
        pltpu.VMEM(wd.shape[1:], BF16),
        pltpu.VMEM(sg.shape, BF16),
        pltpu.VMEM(su.shape, BF16),
        pltpu.VMEM(sd.shape, BF16),
        dma((9,)),
        dma((7, n)),
        dma((nz + 1,)),
        dma((n, nz)),
        dma((n, nz * max(1, most - 1))),
        dma((n, nz)),
        dma((nz,)),
        dma((n, nz)),
        dma((n, 2 * nz)),
        dma((n, nz)),
        dma((n,)),
    ]
    return pl.pallas_call(
        functools.partial(kernel, lay, experts),
        out_shape=jax.ShapeDtypeStruct((rows, width), BF16),
        in_specs=[anyw] * 9,
        out_specs=vmem,
        scratch_shapes=scratch,
        compiler_params=pltpu.CompilerParams(
            collective_id=0, has_side_effects=True, vmem_limit_bytes=67043328
        ),
    )(tokens, ids, rw, wg, wu, wd, sg, su, sd)


def solution(mesh):
    shape = dict(mesh.shape)

    def body(tokens, ids, rw, wg, wu, wd, sg, su, sd):
        experts = shape["expert"] * shape["pair"] * wg.shape[0]
        lay = Layout(shape["expert"], shape["tensor"], tokens.shape[0], tokens.shape[1], experts)
        return per_device(lay, experts, tokens, ids.T, rw.T, wg, wu, wd, sg, su, sd)

    in_specs = (
        P(("groups", "expert", "tensor", "pair"), None),
        P(("groups", "expert", "tensor", "pair"), None),
        P(("groups", "expert", "tensor", "pair"), None),
        P(("expert", "pair"), None, "tensor"),
        P(("expert", "pair"), None, "tensor"),
        P(("expert", "pair"), "tensor", None),
        P(None, ("tensor", "pair")),
        P(None, ("tensor", "pair")),
        P(("tensor", "pair"), None),
    )
    out_specs = P(("groups", "expert", "tensor", "pair"), None)
    return jax.shard_map(body, mesh=mesh, in_specs=in_specs, out_specs=out_specs, check_vma=False)
```

```python
import functools

import jax
import jax.numpy as jnp
from jax import lax
from jax.experimental import pallas as pl
from jax.experimental.pallas import tpu as pltpu
from jax.sharding import PartitionSpec as P

MESH = pl.DeviceIdType.MESH
F32 = jnp.float32
BF16 = jnp.bfloat16


def lanes_for(experts):
    return -(-3 * experts // 128) * 128


def tile_of(width, most):
    for tile in range(min(width, most), 0, -1):
        if width % tile == 0 and (tile % 128 == 0 or tile == width):
            return tile
    return width


class Layout:
    def __init__(self, n_expert, n_tensor, tok_rows, width, experts):
        self.nt = n_tensor
        self.ny = 2 if n_expert % 2 == 0 else 1
        self.nz = n_expert // self.ny
        self.chips = self.ny * self.nt
        self.plane = 2 * self.chips
        self.blocks = self.nz * self.plane
        self.rows, self.width, self.extra = tok_rows, width, lanes_for(experts)
        self.wide, self.cols, self.halves = self.cut(GATHER), self.cut(REDUCE), self.cut(2)
        self.wide[-1] = (self.wide[-1][0], self.wide[-1][1] + self.extra)
        most = max(GATHER, REDUCE)
        self.first = [(self.nt, self.ny)[h % 2] for h in range(most)]
        self.last = [(self.ny, self.nt)[h % 2] for h in range(most)]

    def cut(self, many):
        units = self.width // 128
        ends = [units * h // many * 128 for h in range(many)] + [self.width]
        return [(a, b - a) for a, b in zip(ends[:-1], ends[1:])]

    def sequences(self, z):
        nz = self.nz
        m = jnp.minimum(z, nz - 1 - z)
        side = jnp.where(z <= nz - 1 - z, 1, -1)
        hops, taken = [z], [z]
        for i in range(1, nz):
            near = z + side * ((i + 1) // 2) if i % 2 else z - side * (i // 2)
            hops.append(jnp.where(i <= 2 * m, near, z + side * (i - m)))
            moved = z + side * (i + 1 - m) if i < nz - 1 else z - side * m
            taken.append(jnp.where(m == 0, z + side * i, jnp.where(i < 2 * m, near, moved)))
        return hops, taken


GATHER = 4
REDUCE = 4


def schedule(nz):
    ops = ["A2 0", "R 1", "A1m 1", "A1e 1", "R 2", "A1e 2", "R 3", "A1m 2", "A3 0", "A2 1"]
    ops += [f"R {i}" for i in range(4, nz)]
    ops += ["A1m 3", "W 0", "S 0", "U 0"]
    for i in range(nz):
        ops += [f"A1m {i + 4}", f"A1e {i + 3}", f"A2 {i + 2}", f"A3 {i + 1}", f"L {i - 1}" if i > 1 else "", f"D {i}"]
        ops += [f"W {i + 1}", f"A2 {i + 3}", f"U {i + 1}", "L 0"]
    ops += ["F 1", f"L {nz - 1}"]
    for j in range(2, nz - 1):
        ops += [f"F {j}", f"Z {j - 1}"]
    ops += [f"F {nz - 1}", "F 0", f"Z {nz - 2}", f"Z {nz - 1}", "Z 0"]
    return tidy(ops, nz)


def tidy(ops, nz):
    out = []
    for op in ops:
        if op and op not in out and int(op.split()[1]) < nz:
            out.append(op)
    return [(op.split()[0], int(op.split()[1])) for op in out]


def kernel(lay, experts, tok_in, ids_in, rw_in, wg_in, wu_in, wd_in, sg_in, su_in, sd_in, out,
           tok, part, ids, rw, recvp, recvb, recva, recvz, hid, hs, wg, wu, wd, sg, su, sd,
           load_sem, bulk_send, line_send, line_recv, first_recv, last_recv, swap_recv, pair_recv, b_recv, a_recv, z_recv):
    nz, ny, nt = lay.nz, lay.ny, lay.nt
    rows, width, chips = lay.rows, lay.width, lay.chips
    e_idx, t, p = lax.axis_index("expert"), lax.axis_index("tensor"), lax.axis_index("pair")
    z, y = e_idx // ny, e_idx % ny
    other = 1 - p
    hops, seq = lay.sequences(z)

    def device(z_, y_, t_):
        return {"expert": z_ * ny + y_, "tensor": t_, "pair": p}

    partner = {"expert": e_idx, "tensor": t, "pair": other}
    t_peers = [(t + d) % nt for d in range(1, nt)]
    y_peers = [(y + d) % ny for d in range(1, ny)]

    barrier = pltpu.get_barrier_semaphore()

    def greet(dev):
        pl.semaphore_signal(barrier, inc=1, device_id=dev, device_id_type=MESH)

    for d in range(1, nz):
        greet(device((z + d) % nz, y, t))
    for t_ in t_peers:
        greet(device(z, y, t_))
    for y_ in y_peers:
        greet(device(z, y_, t))
    greet(partner)

    def place(q, z_, y_, t_):
        return ((z_ * 2 + q) * ny + y_) * nt + t_

    cols = [pl.ds(a, n) for a, n in lay.cols]
    wide = [pl.ds(a, n) for a, n in lay.wide]
    halves = [pl.ds(a, n) for a, n in lay.halves]
    gather, reduce = range(len(wide)), range(len(cols))
    slices = range(max(len(wide), len(cols)))
    first_peers = [(t_peers, y_peers)[h % 2] for h in slices]
    last_peers = [(y_peers, t_peers)[h % 2] for h in slices]
    first_at = [(t, y)[h % 2] for h in slices]
    last_at = [(y, t)[h % 2] for h in slices]

    def yt(h, first_, last_):
        return (last_, first_) if h % 2 == 0 else (first_, last_)

    own = place(p, z, y, t)
    first = pltpu.make_async_copy(tok_in, tok.at[own, :, pl.ds(0, width)], load_sem.at[6])
    small = [pltpu.make_async_copy(ids_in, ids, load_sem.at[7]), pltpu.make_async_copy(rw_in, rw, load_sem.at[8])]
    for load in small:
        load.start()
    first.start()
    loads = [
        pltpu.make_async_copy(src, dst, load_sem.at[i])
        for i, (src, dst) in enumerate(
            ((sg_in, sg), (su_in, su), (wg_in.at[0], wg), (wu_in.at[0], wu), (wd_in.at[0], wd), (sd_in, sd))
        )
    ]
    for load in loads:
        load.start()

    for load in small:
        load.wait()
    lane = lax.broadcasted_iota(jnp.int32, (lay.extra, rows), 0)
    pieces = [jnp.zeros(lane.shape, F32) for _ in range(3)]
    for k in range(ids.shape[0]):
        for m in range(3):
            pieces[m] = pieces[m] + jnp.where(lane == ids[k : k + 1, :] + m * experts, rw[k : k + 1, :], 0.0)
    hi = [v.astype(BF16).astype(F32) for v in pieces]
    rest = [v - h for v, h in zip(pieces, hi)]
    mid = [v.astype(BF16).astype(F32) for v in rest]
    low = [v - h for v, h in zip(rest, mid)]
    mixed = (hi[0] + mid[1] + low[2]).astype(BF16)
    eye = (
        lax.broadcasted_iota(jnp.int32, (rows, rows), 0) == lax.broadcasted_iota(jnp.int32, (rows, rows), 1)
    ).astype(F32).astype(BF16)
    turned = lax.dot_general(eye, mixed, (((1,), (1,)), ((), ())), preferred_element_type=F32)
    tok[own, :, pl.ds(width, lay.extra)] = turned.astype(BF16)

    first.wait()
    pl.semaphore_wait(barrier, nt + ny + nz - 2)

    def remote(src, dst, sem_send, sem_recv, dev):
        return pltpu.make_async_remote_copy(
            src_ref=src, dst_ref=dst, send_sem=sem_send, recv_sem=sem_recv, device_id=dev, device_id_type=MESH)

    def got(view, sem_recv):
        remote(view, view, bulk_send.at[0, 0], sem_recv, partner).wait_recv()

    counts = {}

    def send(kind, h, src, dst, sem_recv, dev, blocks=1):
        remote(src, dst, bulk_send.at[kind, h], sem_recv, dev).start()
        counts[kind, h] = counts.get((kind, h), 0) + blocks

    def send_block(kind, h, idx, sem_recv, dev):
        view = tok.at[idx, :, wide[h]]
        send(kind, h, view, view, sem_recv, dev)

    line_sent = []

    def send_line(slot, idx, z_, target):
        ok = (target >= 0) & (target < nz)
        dev = device(target, y, t)

        def whole():
            remote(tok.at[idx], tok.at[idx], line_send.at[slot], line_recv.at[0, 0], dev).wait_send()

        def part_of(h):
            view = tok.at[idx, :, wide[h]]
            copy = remote(view, view, line_send.at[slot], line_recv.at[h, z_], dev)
            if slot in (0, nz):
                pl.when(ok)(copy.start)
            else:
                copy.start()

        line_sent.append((ok, whole))
        return part_of

    def last_sends(h, idx, z_):
        for v in last_peers[h]:
            send_block(0, h, idx, last_recv.at[h, z_], device(z, *yt(h, first_at[h], v)))

    def swap(h, idx, z_):
        send_block(1, h, idx, swap_recv.at[z_], partner)

    def inner(z_):
        target = jnp.where(z_ < z, z + 1, z - 1)
        return target, (target >= 0) & (target < nz)

    def take(i):
        blk = place(p, seq[i], y, t)
        for h in gather:
            got(tok.at[blk, :, wide[h]], line_recv.at[h, seq[i]])

    def relay_step(i):
        z_ = hops[i]
        target, ok = inner(z_)
        blk = place(p, z_, y, t)
        part_of = send_line(i, blk, z_, target)

        def go():
            for h in gather:
                got(tok.at[blk, :, wide[h]], line_recv.at[h, z_])
                part_of(h)

        pl.when(ok)(go)

    def spread(i):
        z_ = seq[i]
        blk = place(p, z_, y, t)
        for h in gather:
            for d, v in enumerate(first_peers[h]):
                send_block(0, h, blk, first_recv.at[h, d * nz + z_], device(z, *yt(h, v, last_at[h])))
        for h in gather:
            last_sends(h, blk, z_)
            swap(h, blk, z_)

    def inner_step(i):
        pl.when(inner(seq[i])[1])(lambda: spread(i))

    def outer_step(i):
        kept = dict(counts)

        def go():
            take(i)
            spread(i)

        pl.when(jnp.logical_not(inner(seq[i])[1]))(go)
        counts.clear()
        counts.update(kept)

    def start_step():
        up, down_ = send_line(0, own, z, z + 1), send_line(nz, own, z, z - 1)
        for h in gather:
            up(h)
            down_(h)
        spread(0)

    def first_step(i):
        z_ = seq[i]
        for h in gather:
            n = lay.first[h]
            for d in range(n - 1):
                f = (first_at[h] + n - 1 - d) % n
                blk = place(p, z_, *yt(h, f, last_at[h]))
                got(tok.at[blk, :, wide[h]], first_recv.at[h, d * nz + z_])
                last_sends(h, blk, z_)
                swap(h, blk, z_)

    def last_step(i):
        z_ = seq[i]
        for h in gather:
            n = lay.first[h] * (lay.last[h] - 1)
            if n:
                got(tok.at[pl.ds(0, n), :, wide[h]], last_recv.at[h, z_])
            for f in [first_at[h]] + first_peers[h]:
                for v in last_peers[h]:
                    swap(h, place(p, z_, *yt(h, f, v)), z_)

    def partner_wait(i):
        got(tok.at[pl.ds(place(other, seq[i], 0, 0), chips)], swap_recv.at[seq[i]])

    def hidden_tiles(x, w1, w2, scale, store):
        tile = tile_of(w1.shape[1], 512)
        for n in range(w1.shape[1] // tile):
            at = pl.ds(n * tile, tile)
            g = jnp.dot(x, w1[:, at], preferred_element_type=F32)
            u = jnp.dot(x, w2[:, at], preferred_element_type=F32)
            h = g / (1.0 + jnp.exp(-g)) * u
            if scale is not None:
                h = h * scale
            store[:, at] = h.astype(BF16)

    group = [place(q, z, y, t_) for q in range(2) for t_ in range(nt)]

    def shared_up(_):
        loads[0].wait()
        loads[1].wait()
        x = jnp.concatenate([tok[idx, :, pl.ds(0, width)] for idx in group], axis=0)
        hidden_tiles(x, sg, su, None, hs)

    mine = e_idx * 2 + p

    def up(i):
        if i == 0:
            loads[2].wait()
            loads[3].wait()
        at = pl.ds(seq[i] * lay.plane, lay.plane)
        extra = tok[at, :, pl.ds(width, lay.extra)].reshape(lay.plane * rows, lay.extra)
        l2 = lax.broadcasted_iota(jnp.int32, extra.shape, 1)
        pick = (l2 == mine) | (l2 == mine + experts) | (l2 == mine + 2 * experts)
        scale = jnp.sum(jnp.where(pick, extra.astype(F32), 0.0), axis=1, keepdims=True)
        hidden_tiles(tok[at, :, pl.ds(0, width)].reshape(lay.plane * rows, width), wg, wu, scale, hid)

    def down(i):
        if i == 0:
            loads[4].wait()
            loads[5].wait()
        z_ = seq[i]
        for g, at in enumerate(halves):
            v = jnp.dot(hid[...], wd[:, at], preferred_element_type=F32)
            part[pl.ds(z_ * lay.plane, lay.plane), :, at] = v.astype(BF16).reshape(lay.plane, rows, lay.halves[g][1])
            if i == 0:
                v = jnp.dot(hs[...], sd[:, at], preferred_element_type=F32)
                for j, idx in enumerate(group):
                    part[idx, :, at] = (part[idx, :, at].astype(F32) + v[j * rows : (j + 1) * rows]).astype(BF16)
            send(2, g, part.at[pl.ds(place(other, z_, 0, 0), chips), :, at],
                 recvp.at[pl.ds(z_ * chips, chips), :, at], pair_recv.at[g, z_], partner, chips)

    def buf_b(h, d, z_, f):
        return recvb.at[(d * nz + z_) * lay.first[h] + f, :, cols[h]]

    def buf_a(h, d, z_):
        return recva.at[d * nz + z_, :, cols[h]]

    def add_into(h, idx, others):
        v = part[idx, :, cols[h]].astype(F32)
        for ref in others:
            v = v + ref[...].astype(F32)
        part[idx, :, cols[h]] = v.astype(BF16)

    def mine_of(z_, y_, t_, h):
        return recvp.at[(z_ * ny + y_) * nt + t_, :, cols[h]]

    starts = [0, len(cols) // 2]

    def sums_last(i):
        z_ = seq[i]
        for h in reduce:
            if h in starts:
                g = starts.index(h)
                got(recvp.at[pl.ds(z_ * chips, chips), :, halves[g]], pair_recv.at[g, z_])
            for k, f in enumerate(first_peers[h] + [first_at[h]]):
                here = int(k == lay.first[h] - 1)
                for d, v in enumerate(last_peers[h]):
                    y_, t_ = yt(h, f, v)
                    idx = place(p, z_, y_, t_)
                    add_into(h, idx, [mine_of(z_, y_, t_, h)])
                    send(3, h, part.at[idx, :, cols[h]], buf_b(h, d, z_, f), (a_recv if here else b_recv).at[h, z_],
                         device(z, *yt(h, first_at[h], v)))

    def collect_last(h, z_, f):
        y_, t_ = yt(h, f, last_at[h])
        return place(p, z_, y_, t_), [mine_of(z_, y_, t_, h)] + [buf_b(h, d, z_, f) for d in range(lay.last[h] - 1)]

    def sums_first(i):
        z_ = seq[i]
        for h in reduce:
            n = (lay.first[h] - 1) * (lay.last[h] - 1)
            if n:
                got(recvb.at[pl.ds(0, n), :, cols[h]], b_recv.at[h, z_])
            for d, f in enumerate(first_peers[h]):
                idx, refs = collect_last(h, z_, f)
                add_into(h, idx, refs)
                send(3, h, part.at[idx, :, cols[h]], buf_a(h, d, z_), a_recv.at[h, z_], device(z, *yt(h, f, last_at[h])))

    def sums_line(i):
        z_ = seq[i]
        for h in reduce:
            n = lay.last[h] + lay.first[h] - 2
            if n:
                got(part.at[pl.ds(0, n), :, cols[h]], a_recv.at[h, z_])
            idx, refs = collect_last(h, z_, first_at[h])
            add_into(h, idx, refs + [buf_a(h, d, z_) for d in range(lay.first[h] - 1)])
            if i:
                slot = (z_ - z + nz) % nz - 1
                send(3, h, part.at[idx, :, cols[h]], recvz.at[slot, :, cols[h]], z_recv.at[h], device(z_, y, t))

    start_step()
    steps = {
        "R": relay_step, "A1m": inner_step, "A1e": outer_step, "A2": first_step, "A3": last_step, "W": partner_wait, "S": shared_up, "U": up, "D": down,
        "L": sums_last, "F": sums_first, "Z": sums_line,
    }
    for name, i in schedule(nz):
        steps[name](i)

    for h in reduce:
        if nz > 1:
            got(recvz.at[pl.ds(0, nz - 1), :, cols[h]], z_recv.at[h])
        v = part[own, :, cols[h]].astype(F32)
        for d in range(nz - 1):
            v = v + recvz[d, :, cols[h]].astype(F32)
        out[:, cols[h]] = v.astype(BF16)
    for ok, whole in line_sent:
        pl.when(ok)(whole)
    for (kind, h), n in counts.items():
        view = (tok if kind < 2 else part).at[pl.ds(0, n), :, (wide, wide, halves, cols)[kind][h]]
        remote(view, view, bulk_send.at[kind, h], z_recv.at[h], partner).wait_send()


def per_device(lay, experts, tokens, ids, rw, wg, wu, wd, sg, su, sd):
    rows, width = tokens.shape
    nz, ny, nt = lay.nz, lay.ny, lay.nt
    hidden, shared = wg.shape[2], sg.shape[1]
    n, most = max(GATHER, REDUCE), max(nt, ny)
    many_b = max(1, max((lay.last[h] - 1) * lay.first[h] for h in range(n)) * nz)
    many_a = max(1, (most - 1) * nz)
    vmem = pl.BlockSpec(memory_space=pltpu.VMEM)
    anyw = pl.BlockSpec(memory_space=pl.ANY)
    dma = pltpu.SemaphoreType.DMA
    scratch = [
        pltpu.VMEM((lay.blocks, rows, width + lay.extra), BF16),
        pltpu.VMEM((lay.blocks, rows, width), BF16),
        pltpu.VMEM(ids.shape, jnp.int32),
        pltpu.VMEM(rw.shape, F32),
        pltpu.VMEM((lay.blocks // 2, rows, width), BF16),
        pltpu.VMEM((many_b, rows, width), BF16),
        pltpu.VMEM((many_a, rows, width), BF16),
        pltpu.VMEM((max(1, nz - 1), rows, width), BF16),
        pltpu.VMEM((lay.plane * rows, hidden), BF16),
        pltpu.VMEM((2 * nt * rows, shared), BF16),
        pltpu.VMEM(wg.shape[1:], BF16),
        pltpu.VMEM(wu.shape[1:], BF16),
        pltpu.VMEM(wd.shape[1:], BF16),
        pltpu.VMEM(sg.shape, BF16),
        pltpu.VMEM(su.shape, BF16),
        pltpu.VMEM(sd.shape, BF16),
        dma((9,)),
        dma((4, n)),
        dma((nz + 1,)),
        dma((GATHER, nz)),
        dma((GATHER, nz * max(1, most - 1))),
        dma((GATHER, nz)),
        dma((nz,)),
        dma((2, nz)),
        dma((REDUCE, nz)),
        dma((REDUCE, nz)),
        dma((REDUCE,)),
    ]
    return pl.pallas_call(
        functools.partial(kernel, lay, experts),
        out_shape=jax.ShapeDtypeStruct((rows, width), BF16),
        in_specs=[anyw] * 9,
        out_specs=vmem,
        scratch_shapes=scratch,
        compiler_params=pltpu.CompilerParams(
            collective_id=0, has_side_effects=True, vmem_limit_bytes=67043328
        ),
    )(tokens, ids, rw, wg, wu, wd, sg, su, sd)


def solution(mesh):
    shape = dict(mesh.shape)

    def body(tokens, ids, rw, wg, wu, wd, sg, su, sd):
        experts = shape["expert"] * shape["pair"] * wg.shape[0]
        lay = Layout(shape["expert"], shape["tensor"], tokens.shape[0], tokens.shape[1], experts)
        return per_device(lay, experts, tokens, ids.T, rw.T, wg, wu, wd, sg, su, sd)

    in_specs = (
        P(("groups", "expert", "tensor", "pair"), None),
        P(("groups", "expert", "tensor", "pair"), None),
        P(("groups", "expert", "tensor", "pair"), None),
        P(("expert", "pair"), None, "tensor"),
        P(("expert", "pair"), None, "tensor"),
        P(("expert", "pair"), "tensor", None),
        P(None, ("tensor", "pair")),
        P(None, ("tensor", "pair")),
        P(("tensor", "pair"), None),
    )
    out_specs = P(("groups", "expert", "tensor", "pair"), None)
    return jax.shard_map(body, mesh=mesh, in_specs=in_specs, out_specs=out_specs, check_vma=False)
```

```python
import functools

import jax
import jax.numpy as jnp
from jax import lax
from jax.experimental import pallas as pl
from jax.experimental.pallas import tpu as pltpu
from jax.sharding import PartitionSpec as P

MESH = pl.DeviceIdType.MESH
F32 = jnp.float32
BF16 = jnp.bfloat16


def lanes_for(experts):
    return -(-3 * experts // 128) * 128


def tile_of(width, most):
    for tile in range(min(width, most), 0, -1):
        if width % tile == 0 and (tile % 128 == 0 or tile == width):
            return tile
    return width


class Layout:
    def __init__(self, n_expert, n_tensor, tok_rows, width, experts):
        self.nt = n_tensor
        self.ny = 2 if n_expert % 2 == 0 else 1
        self.nz = n_expert // self.ny
        self.chips = self.ny * self.nt
        self.plane = 2 * self.chips
        self.blocks = self.nz * self.plane
        self.rows, self.width, self.extra = tok_rows, width, lanes_for(experts)
        self.wide, self.cols, self.halves = self.cut(GATHER), self.cut(REDUCE), self.cut(2)
        self.wide[-1] = (self.wide[-1][0], self.wide[-1][1] + self.extra)
        most = max(GATHER, REDUCE)
        self.first = [(self.nt, self.ny)[h % 2] for h in range(most)]
        self.last = [(self.ny, self.nt)[h % 2] for h in range(most)]

    def cut(self, many):
        units = self.width // 128
        ends = [units * h // many * 128 for h in range(many)] + [self.width]
        return [(a, b - a) for a, b in zip(ends[:-1], ends[1:])]

    def sequences(self, z):
        nz = self.nz
        m = jnp.minimum(z, nz - 1 - z)
        side = jnp.where(z <= nz - 1 - z, 1, -1)
        hops, taken = [z], [z]
        for i in range(1, nz):
            near = z + side * ((i + 1) // 2) if i % 2 else z - side * (i // 2)
            hops.append(jnp.where(i <= 2 * m, near, z + side * (i - m)))
            moved = z + side * (i + 1 - m) if i < nz - 1 else z - side * m
            taken.append(jnp.where(m == 0, z + side * i, jnp.where(i < 2 * m, near, moved)))
        return hops, taken


GATHER = 4
REDUCE = 4
CROSS = 2


def schedule(nz):
    ops = ["A2 0", "R 1", "A1m 1", "A1e 1", "R 2", "X 0", "A1e 2", "R 3", "A1m 2"]
    ops += [f"R {i}" for i in range(4, nz)]
    ops += ["A3 0", "RB 1", "RB 2", "Bm 1", "Be 1", "A2 1", "A1m 3", "W 0", "S 0", "U 0"]
    for i in range(nz):
        ops += [f"A1m {i + 4}", f"A1e {i + 3}", f"RB {i + 3}", f"A2 {i + 2}", f"Bm {i + 2}", f"Be {i + 2}", f"Bm {i + 3}" if i + 4 >= nz else ""]
        ops += [f"A3 {i + 1}", f"L {i - 1}" if i > 1 else "", f"D {i}"]
        ops += [f"W {i + 1}", f"A2 {i + 3}", f"U {i + 1}", f"Be {i + 3}", "L 0"]
    ops += ["F 1", f"L {nz - 1}"]
    for j in range(2, nz - 1):
        ops += [f"F {j}", f"Z {j - 1}"]
    ops += [f"F {nz - 1}", "F 0", f"Z {nz - 2}", f"Z {nz - 1}", "Z 0"]
    return tidy(ops, nz)


def tidy(ops, nz):
    out = []
    for op in ops:
        if op and op not in out and int(op.split()[1]) < nz:
            out.append(op)
    return [(op.split()[0], int(op.split()[1])) for op in out]


def kernel(lay, experts, tok_in, ids_in, rw_in, wg_in, wu_in, wd_in, sg_in, su_in, sd_in, out,
           tok, part, ids, rw, recvp, recvb, recva, recvz, hid, hs, wg, wu, wd, sg, su, sd,
           load_sem, bulk_send, line_send, line_recv, first_recv, last_recv, swap_recv, pair_recv, b_recv, a_recv, z_recv, cross_send, cross_recv):
    nz, ny, nt = lay.nz, lay.ny, lay.nt
    rows, width, chips = lay.rows, lay.width, lay.chips
    e_idx, t, p = lax.axis_index("expert"), lax.axis_index("tensor"), lax.axis_index("pair")
    z, y = e_idx // ny, e_idx % ny
    other = 1 - p
    hops, seq = lay.sequences(z)

    def device(z_, y_, t_):
        return {"expert": z_ * ny + y_, "tensor": t_, "pair": p}

    partner = {"expert": e_idx, "tensor": t, "pair": other}
    t_peers = [(t + d) % nt for d in range(1, nt)]
    y_peers = [(y + d) % ny for d in range(1, ny)]

    barrier = pltpu.get_barrier_semaphore()

    def greet(dev):
        pl.semaphore_signal(barrier, inc=1, device_id=dev, device_id_type=MESH)

    for d in range(1, nz):
        greet(device((z + d) % nz, y, t))
    for t_ in t_peers:
        greet(device(z, y, t_))
    for y_ in y_peers:
        greet(device(z, y_, t))
    greet(partner)

    def place(q, z_, y_, t_):
        return ((z_ * 2 + q) * ny + y_) * nt + t_

    cols = [pl.ds(a, n) for a, n in lay.cols]
    wide = [pl.ds(a, n) for a, n in lay.wide]
    halves = [pl.ds(a, n) for a, n in lay.halves]
    gather, reduce = range(len(wide)), range(len(cols))
    slices = range(max(len(wide), len(cols)))
    first_peers = [(t_peers, y_peers)[h % 2] for h in slices]
    last_peers = [(y_peers, t_peers)[h % 2] for h in slices]
    first_at = [(t, y)[h % 2] for h in slices]
    last_at = [(y, t)[h % 2] for h in slices]

    def yt(h, first_, last_):
        return (last_, first_) if h % 2 == 0 else (first_, last_)

    own = place(p, z, y, t)
    first = pltpu.make_async_copy(tok_in, tok.at[own, :, pl.ds(0, width)], load_sem.at[6])
    small = [pltpu.make_async_copy(ids_in, ids, load_sem.at[7]), pltpu.make_async_copy(rw_in, rw, load_sem.at[8])]
    for load in small:
        load.start()
    first.start()
    loads = [
        pltpu.make_async_copy(src, dst, load_sem.at[i])
        for i, (src, dst) in enumerate(
            ((sg_in, sg), (su_in, su), (wg_in.at[0], wg), (wu_in.at[0], wu), (wd_in.at[0], wd), (sd_in, sd))
        )
    ]
    for load in loads:
        load.start()

    for load in small:
        load.wait()
    lane = lax.broadcasted_iota(jnp.int32, (lay.extra, rows), 0)
    pieces = [jnp.zeros(lane.shape, F32) for _ in range(3)]
    for k in range(ids.shape[0]):
        for m in range(3):
            pieces[m] = pieces[m] + jnp.where(lane == ids[k : k + 1, :] + m * experts, rw[k : k + 1, :], 0.0)
    hi = [v.astype(BF16).astype(F32) for v in pieces]
    rest = [v - h for v, h in zip(pieces, hi)]
    mid = [v.astype(BF16).astype(F32) for v in rest]
    low = [v - h for v, h in zip(rest, mid)]
    mixed = (hi[0] + mid[1] + low[2]).astype(BF16)
    eye = (
        lax.broadcasted_iota(jnp.int32, (rows, rows), 0) == lax.broadcasted_iota(jnp.int32, (rows, rows), 1)
    ).astype(F32).astype(BF16)
    turned = lax.dot_general(eye, mixed, (((1,), (1,)), ((), ())), preferred_element_type=F32)
    tok[own, :, pl.ds(width, lay.extra)] = turned.astype(BF16)

    first.wait()
    pl.semaphore_wait(barrier, nt + ny + nz - 2)

    def remote(src, dst, sem_send, sem_recv, dev):
        return pltpu.make_async_remote_copy(
            src_ref=src, dst_ref=dst, send_sem=sem_send, recv_sem=sem_recv, device_id=dev, device_id_type=MESH)

    def got(view, sem_recv):
        remote(view, view, bulk_send.at[0, 0], sem_recv, partner).wait_recv()

    counts = {}

    def send(kind, h, src, dst, sem_recv, dev, blocks=1):
        remote(src, dst, bulk_send.at[kind, h], sem_recv, dev).start()
        counts[kind, h] = counts.get((kind, h), 0) + blocks

    def send_block(kind, h, idx, sem_recv, dev):
        view = tok.at[idx, :, wide[h]]
        send(kind, h, view, view, sem_recv, dev)

    line_sent = []

    def send_line(slot, idx, z_, target):
        ok = (target >= 0) & (target < nz)
        dev = device(target, y, t)

        def whole():
            remote(tok.at[idx], tok.at[idx], line_send.at[slot], line_recv.at[0, 0], dev).wait_send()

        def part_of(h):
            view = tok.at[idx, :, wide[h]]
            copy = remote(view, view, line_send.at[slot], line_recv.at[h, z_], dev)
            if slot in (0, nz):
                pl.when(ok)(copy.start)
            else:
                copy.start()

        line_sent.append((ok, whole))
        return part_of

    def last_sends(h, idx, z_):
        for v in last_peers[h]:
            send_block(0, h, idx, last_recv.at[h, z_], device(z, *yt(h, first_at[h], v)))

    def swap(h, idx, z_):
        send_block(1, h, idx, swap_recv.at[z_], partner)

    def inner(z_):
        target = jnp.where(z_ < z, z + 1, z - 1)
        return target, (target >= 0) & (target < nz)

    def take(i):
        blk = place(p, seq[i], y, t)
        for h in gather:
            got(tok.at[blk, :, wide[h]], line_recv.at[h, seq[i]])

    def relay_step(i):
        z_ = hops[i]
        target, ok = inner(z_)
        blk = place(p, z_, y, t)
        part_of = send_line(i, blk, z_, target)

        def go():
            for h in gather:
                got(tok.at[blk, :, wide[h]], line_recv.at[h, z_])
                part_of(h)

        pl.when(ok)(go)

    crossing = list(gather)[len(gather) - CROSS :]
    cross_sent = []

    def send_cross(h, slot, z_, target):
        c = h - crossing[0]
        ok = (target >= 0) & (target < nz)
        dev = device(target, y, t)

        def copies():
            for f in first_peers[h]:
                view = tok.at[place(p, z_, *yt(h, f, last_at[h])), :, wide[h]]
                yield remote(view, view, cross_send.at[c, slot], cross_recv.at[c, z_], dev)

        def go():
            for copy in copies():
                copy.start()

        def drained():
            if lay.first[h] > 1:
                view = tok.at[pl.ds(0, lay.first[h] - 1), :, wide[h]]
                remote(view, view, cross_send.at[c, slot], cross_recv.at[c, z_], dev).wait_send()

        cross_sent.append((ok, drained))
        return ok, go

    def start_cross(_):
        for h in crossing:
            for slot, target in ((0, z + 1), (nz, z - 1)):
                ok, start = send_cross(h, slot, z, target)
                pl.when(ok)(start)

    def take_cross(h, z_):
        if lay.first[h] > 1:
            got(tok.at[pl.ds(0, lay.first[h] - 1), :, wide[h]], cross_recv.at[h - crossing[0], z_])

    def relay_cross(k):
        z_ = hops[k]
        target, ok = inner(z_)
        sends = [(h, send_cross(h, k, z_, target)[1]) for h in crossing]

        def go():
            for h, start in sends:
                take_cross(h, z_)
                start()

        pl.when(ok)(go)

    def spread_cross(h, z_):
        for f in first_peers[h]:
            blk = place(p, z_, *yt(h, f, last_at[h]))
            last_sends(h, blk, z_)
            swap(h, blk, z_)

    def inner_cross(i):
        def go():
            for h in crossing:
                spread_cross(h, seq[i])

        pl.when(inner(seq[i])[1])(go)

    def outer_cross(i):
        kept = dict(counts)

        def go():
            for h in crossing:
                take_cross(h, seq[i])
                spread_cross(h, seq[i])

        pl.when(jnp.logical_not(inner(seq[i])[1]))(go)
        counts.clear()
        counts.update(kept)

    def spread(i):
        z_ = seq[i]
        blk = place(p, z_, y, t)
        for h in gather:
            if i and h in crossing:
                continue
            for d, v in enumerate(first_peers[h]):
                send_block(0, h, blk, first_recv.at[h, d * nz + z_], device(z, *yt(h, v, last_at[h])))
        for h in gather:
            last_sends(h, blk, z_)
            swap(h, blk, z_)

    def inner_step(i):
        pl.when(inner(seq[i])[1])(lambda: spread(i))

    def outer_step(i):
        kept = dict(counts)

        def go():
            take(i)
            spread(i)

        pl.when(jnp.logical_not(inner(seq[i])[1]))(go)
        counts.clear()
        counts.update(kept)

    def start_step():
        up, down_ = send_line(0, own, z, z + 1), send_line(nz, own, z, z - 1)
        for h in gather:
            up(h)
            down_(h)
        spread(0)

    def first_step(i):
        z_ = seq[i]
        for h in gather:
            n = lay.first[h]
            if i and h in crossing:
                continue
            onward = h in crossing
            for d in range(n - 1):
                f = (first_at[h] + n - 1 - d) % n
                blk = place(p, z_, *yt(h, f, last_at[h]))
                got(tok.at[blk, :, wide[h]], first_recv.at[h, d * nz + z_])
                if not onward:
                    last_sends(h, blk, z_)
                    swap(h, blk, z_)
            if onward:
                spread_cross(h, z_)

    def last_step(i):
        z_ = seq[i]
        for h in gather:
            n = lay.first[h] * (lay.last[h] - 1)
            if n:
                got(tok.at[pl.ds(0, n), :, wide[h]], last_recv.at[h, z_])
            for f in [first_at[h]] + first_peers[h]:
                for v in last_peers[h]:
                    swap(h, place(p, z_, *yt(h, f, v)), z_)

    def partner_wait(i):
        got(tok.at[pl.ds(place(other, seq[i], 0, 0), chips)], swap_recv.at[seq[i]])

    def hidden_tiles(x, w1, w2, scale, store):
        tile = tile_of(w1.shape[1], 512)
        for n in range(w1.shape[1] // tile):
            at = pl.ds(n * tile, tile)
            g = jnp.dot(x, w1[:, at], preferred_element_type=F32)
            u = jnp.dot(x, w2[:, at], preferred_element_type=F32)
            h = g / (1.0 + jnp.exp(-g)) * u
            if scale is not None:
                h = h * scale
            store[:, at] = h.astype(BF16)

    group = [place(q, z, y, t_) for q in range(2) for t_ in range(nt)]

    def shared_up(_):
        loads[0].wait()
        loads[1].wait()
        x = jnp.concatenate([tok[idx, :, pl.ds(0, width)] for idx in group], axis=0)
        hidden_tiles(x, sg, su, None, hs)

    mine = e_idx * 2 + p

    def up(i):
        if i == 0:
            loads[2].wait()
            loads[3].wait()
        at = pl.ds(seq[i] * lay.plane, lay.plane)
        extra = tok[at, :, pl.ds(width, lay.extra)].reshape(lay.plane * rows, lay.extra)
        l2 = lax.broadcasted_iota(jnp.int32, extra.shape, 1)
        pick = (l2 == mine) | (l2 == mine + experts) | (l2 == mine + 2 * experts)
        scale = jnp.sum(jnp.where(pick, extra.astype(F32), 0.0), axis=1, keepdims=True)
        hidden_tiles(tok[at, :, pl.ds(0, width)].reshape(lay.plane * rows, width), wg, wu, scale, hid)

    def down(i):
        if i == 0:
            loads[4].wait()
            loads[5].wait()
        z_ = seq[i]
        for g, at in enumerate(halves):
            v = jnp.dot(hid[...], wd[:, at], preferred_element_type=F32)
            part[pl.ds(z_ * lay.plane, lay.plane), :, at] = v.astype(BF16).reshape(lay.plane, rows, lay.halves[g][1])
            if i == 0:
                v = jnp.dot(hs[...], sd[:, at], preferred_element_type=F32)
                for j, idx in enumerate(group):
                    part[idx, :, at] = (part[idx, :, at].astype(F32) + v[j * rows : (j + 1) * rows]).astype(BF16)
            send(2, g, part.at[pl.ds(place(other, z_, 0, 0), chips), :, at],
                 recvp.at[pl.ds(z_ * chips, chips), :, at], pair_recv.at[g, z_], partner, chips)

    def buf_b(h, d, z_, f):
        return recvb.at[(d * nz + z_) * lay.first[h] + f, :, cols[h]]

    def buf_a(h, d, z_):
        return recva.at[d * nz + z_, :, cols[h]]

    def add_into(h, idx, others):
        v = part[idx, :, cols[h]].astype(F32)
        for ref in others:
            v = v + ref[...].astype(F32)
        part[idx, :, cols[h]] = v.astype(BF16)

    def mine_of(z_, y_, t_, h):
        return recvp.at[(z_ * ny + y_) * nt + t_, :, cols[h]]

    starts = [0, len(cols) // 2]

    def sums_last(i):
        z_ = seq[i]
        for h in reduce:
            if h in starts:
                g = starts.index(h)
                got(recvp.at[pl.ds(z_ * chips, chips), :, halves[g]], pair_recv.at[g, z_])
            for k, f in enumerate(first_peers[h] + [first_at[h]]):
                here = int(k == lay.first[h] - 1)
                for d, v in enumerate(last_peers[h]):
                    y_, t_ = yt(h, f, v)
                    idx = place(p, z_, y_, t_)
                    add_into(h, idx, [mine_of(z_, y_, t_, h)])
                    send(3, h, part.at[idx, :, cols[h]], buf_b(h, d, z_, f), (a_recv if here else b_recv).at[h, z_],
                         device(z, *yt(h, first_at[h], v)))

    def collect_last(h, z_, f):
        y_, t_ = yt(h, f, last_at[h])
        return place(p, z_, y_, t_), [mine_of(z_, y_, t_, h)] + [buf_b(h, d, z_, f) for d in range(lay.last[h] - 1)]

    def sums_first(i):
        z_ = seq[i]
        for h in reduce:
            n = (lay.first[h] - 1) * (lay.last[h] - 1)
            if n:
                got(recvb.at[pl.ds(0, n), :, cols[h]], b_recv.at[h, z_])
            for d, f in enumerate(first_peers[h]):
                idx, refs = collect_last(h, z_, f)
                add_into(h, idx, refs)
                send(3, h, part.at[idx, :, cols[h]], buf_a(h, d, z_), a_recv.at[h, z_], device(z, *yt(h, f, last_at[h])))

    def sums_line(i):
        z_ = seq[i]
        for h in reduce:
            n = lay.last[h] + lay.first[h] - 2
            if n:
                got(part.at[pl.ds(0, n), :, cols[h]], a_recv.at[h, z_])
            idx, refs = collect_last(h, z_, first_at[h])
            add_into(h, idx, refs + [buf_a(h, d, z_) for d in range(lay.first[h] - 1)])
            if i:
                slot = (z_ - z + nz) % nz - 1
                send(3, h, part.at[idx, :, cols[h]], recvz.at[slot, :, cols[h]], z_recv.at[h], device(z_, y, t))

    start_step()
    steps = {
        "R": relay_step, "X": start_cross, "RB": relay_cross, "Bm": inner_cross, "Be": outer_cross, "A1m": inner_step, "A1e": outer_step, "A2": first_step, "A3": last_step, "W": partner_wait, "S": shared_up, "U": up, "D": down,
        "L": sums_last, "F": sums_first, "Z": sums_line,
    }
    for name, i in schedule(nz):
        steps[name](i)

    for h in reduce:
        if nz > 1:
            got(recvz.at[pl.ds(0, nz - 1), :, cols[h]], z_recv.at[h])
        v = part[own, :, cols[h]].astype(F32)
        for d in range(nz - 1):
            v = v + recvz[d, :, cols[h]].astype(F32)
        out[:, cols[h]] = v.astype(BF16)
    for ok, whole in line_sent + cross_sent:
        pl.when(ok)(whole)
    for (kind, h), n in counts.items():
        view = (tok if kind < 2 else part).at[pl.ds(0, n), :, (wide, wide, halves, cols)[kind][h]]
        remote(view, view, bulk_send.at[kind, h], z_recv.at[h], partner).wait_send()


def per_device(lay, experts, tokens, ids, rw, wg, wu, wd, sg, su, sd):
    rows, width = tokens.shape
    nz, ny, nt = lay.nz, lay.ny, lay.nt
    hidden, shared = wg.shape[2], sg.shape[1]
    n, most = max(GATHER, REDUCE), max(nt, ny)
    many_b = max(1, max((lay.last[h] - 1) * lay.first[h] for h in range(n)) * nz)
    many_a = max(1, (most - 1) * nz)
    vmem = pl.BlockSpec(memory_space=pltpu.VMEM)
    anyw = pl.BlockSpec(memory_space=pl.ANY)
    dma = pltpu.SemaphoreType.DMA
    scratch = [
        pltpu.VMEM((lay.blocks, rows, width + lay.extra), BF16),
        pltpu.VMEM((lay.blocks, rows, width), BF16),
        pltpu.VMEM(ids.shape, jnp.int32),
        pltpu.VMEM(rw.shape, F32),
        pltpu.VMEM((lay.blocks // 2, rows, width), BF16),
        pltpu.VMEM((many_b, rows, width), BF16),
        pltpu.VMEM((many_a, rows, width), BF16),
        pltpu.VMEM((max(1, nz - 1), rows, width), BF16),
        pltpu.VMEM((lay.plane * rows, hidden), BF16),
        pltpu.VMEM((2 * nt * rows, shared), BF16),
        pltpu.VMEM(wg.shape[1:], BF16),
        pltpu.VMEM(wu.shape[1:], BF16),
        pltpu.VMEM(wd.shape[1:], BF16),
        pltpu.VMEM(sg.shape, BF16),
        pltpu.VMEM(su.shape, BF16),
        pltpu.VMEM(sd.shape, BF16),
        dma((9,)),
        dma((4, n)),
        dma((nz + 1,)),
        dma((GATHER, nz)),
        dma((GATHER, nz * max(1, most - 1))),
        dma((GATHER, nz)),
        dma((nz,)),
        dma((2, nz)),
        dma((REDUCE, nz)),
        dma((REDUCE, nz)),
        dma((REDUCE,)),
        dma((max(1, CROSS), nz + 1)),
        dma((max(1, CROSS), nz)),
    ]
    return pl.pallas_call(
        functools.partial(kernel, lay, experts),
        out_shape=jax.ShapeDtypeStruct((rows, width), BF16),
        in_specs=[anyw] * 9,
        out_specs=vmem,
        scratch_shapes=scratch,
        compiler_params=pltpu.CompilerParams(
            collective_id=0, has_side_effects=True, vmem_limit_bytes=67043328
        ),
    )(tokens, ids, rw, wg, wu, wd, sg, su, sd)


def solution(mesh):
    shape = dict(mesh.shape)

    def body(tokens, ids, rw, wg, wu, wd, sg, su, sd):
        experts = shape["expert"] * shape["pair"] * wg.shape[0]
        lay = Layout(shape["expert"], shape["tensor"], tokens.shape[0], tokens.shape[1], experts)
        return per_device(lay, experts, tokens, ids.T, rw.T, wg, wu, wd, sg, su, sd)

    in_specs = (
        P(("groups", "expert", "tensor", "pair"), None),
        P(("groups", "expert", "tensor", "pair"), None),
        P(("groups", "expert", "tensor", "pair"), None),
        P(("expert", "pair"), None, "tensor"),
        P(("expert", "pair"), None, "tensor"),
        P(("expert", "pair"), "tensor", None),
        P(None, ("tensor", "pair")),
        P(None, ("tensor", "pair")),
        P(("tensor", "pair"), None),
    )
    out_specs = P(("groups", "expert", "tensor", "pair"), None)
    return jax.shard_map(body, mesh=mesh, in_specs=in_specs, out_specs=out_specs, check_vma=False)
```

```python
import functools

import jax
import jax.numpy as jnp
from jax import lax
from jax.experimental import pallas as pl
from jax.experimental.pallas import tpu as pltpu
from jax.sharding import PartitionSpec as P

MESH = pl.DeviceIdType.MESH
F32 = jnp.float32
BF16 = jnp.bfloat16


def lanes_for(experts):
    return -(-3 * experts // 128) * 128


def tile_of(width, most):
    for tile in range(min(width, most), 0, -1):
        if width % tile == 0 and (tile % 128 == 0 or tile == width):
            return tile
    return width


class Layout:
    def __init__(self, n_expert, n_tensor, tok_rows, width, experts):
        self.nt = n_tensor
        self.ny = 2 if n_expert % 2 == 0 else 1
        self.nz = n_expert // self.ny
        self.chips = self.ny * self.nt
        self.plane = 2 * self.chips
        self.blocks = self.nz * self.plane
        self.rows, self.width, self.extra = tok_rows, width, lanes_for(experts)
        self.wide, self.cols, self.halves = self.cut(GATHER), self.cut(REDUCE), self.cut(2)
        self.wide[-1] = (self.wide[-1][0], self.wide[-1][1] + self.extra)
        most = max(GATHER, REDUCE)
        self.first = [(self.nt, self.ny)[h % 2] for h in range(most)]
        self.last = [(self.ny, self.nt)[h % 2] for h in range(most)]

    def cut(self, many):
        units = self.width // 128
        ends = [units * h // many * 128 for h in range(many)] + [self.width]
        return [(a, b - a) for a, b in zip(ends[:-1], ends[1:])]

    def sequences(self, z):
        nz = self.nz
        m = jnp.minimum(z, nz - 1 - z)
        side = jnp.where(z <= nz - 1 - z, 1, -1)
        hops, taken = [z], [z]
        for i in range(1, nz):
            near = z + side * ((i + 1) // 2) if i % 2 else z - side * (i // 2)
            hops.append(jnp.where(i <= 2 * m, near, z + side * (i - m)))
            moved = z + side * (i + 1 - m) if i < nz - 1 else z - side * m
            taken.append(jnp.where(m == 0, z + side * i, jnp.where(i < 2 * m, near, moved)))
        return hops, taken


GATHER = 4
REDUCE = 4
CROSS = 2


def schedule(nz):
    ops = ["A2 0", "R 1", "A1m 1", "A1e 1", "R 2", "X 0", "A1e 2", "R 3", "A1m 2"]
    ops += [f"R {i}" for i in range(4, nz)]
    ops += ["A3 0", "RB 1", "RB 2", "Bm 1", "Be 1", "A2 1", "A1m 3", "W 0", "S 0", "U 0"]
    for i in range(nz):
        ops += [f"A1m {i + 4}", f"A1e {i + 3}", f"RB {i + 3}", f"A2 {i + 2}", f"Bm {i + 2}", f"Be {i + 2}", f"Bm {i + 3}" if i + 4 >= nz else ""]
        ops += [f"A3 {i + 1}", f"L {i - 1}" if i > 1 else "", f"D {i}"]
        ops += [f"W {i + 1}", f"A2 {i + 3}", f"U {i + 1}", f"Be {i + 3}", "L 0"]
    ops += ["F 1", f"L {nz - 1}"]
    for j in range(2, nz - 1):
        ops += [f"F {j}", f"Z {j - 1}"]
    ops += [f"F {nz - 1}", "F 0", f"Z {nz - 2}", f"Z {nz - 1}", "Z 0"]
    return tidy(ops, nz)


def tidy(ops, nz):
    out = []
    for op in ops:
        if op and op not in out and int(op.split()[1]) < nz:
            out.append(op)
    return [(op.split()[0], int(op.split()[1])) for op in out]


def kernel(lay, experts, tok_in, ids_in, rw_in, wg_in, wu_in, wd_in, sg_in, su_in, sd_in, out,
           tok, part, ids, rw, recvp, recvb, recva, recvz, hid, hs, wg, wu, wd, sg, su, sd,
           load_sem, bulk_send, line_send, line_recv, first_recv, last_recv, swap_recv, pair_recv, b_recv, a_recv, z_recv, cross_send, cross_recv, result, store_sem):
    nz, ny, nt = lay.nz, lay.ny, lay.nt
    rows, width, chips = lay.rows, lay.width, lay.chips
    e_idx, t, p = lax.axis_index("expert"), lax.axis_index("tensor"), lax.axis_index("pair")
    z, y = e_idx // ny, e_idx % ny
    other = 1 - p
    hops, seq = lay.sequences(z)

    def device(z_, y_, t_):
        return {"expert": z_ * ny + y_, "tensor": t_, "pair": p}

    partner = {"expert": e_idx, "tensor": t, "pair": other}
    t_peers = [(t + d) % nt for d in range(1, nt)]
    y_peers = [(y + d) % ny for d in range(1, ny)]

    barrier = pltpu.get_barrier_semaphore()

    def greet(dev):
        pl.semaphore_signal(barrier, inc=1, device_id=dev, device_id_type=MESH)

    for z_ in (z + 1, z - 1):
        pl.when((z_ >= 0) & (z_ < nz))(functools.partial(greet, device(z_, y, t)))
    for t_ in t_peers:
        greet(device(z, y, t_))
    for y_ in y_peers:
        greet(device(z, y_, t))
    greet(partner)

    def place(q, z_, y_, t_):
        return ((z_ * 2 + q) * ny + y_) * nt + t_

    cols = [pl.ds(a, n) for a, n in lay.cols]
    wide = [pl.ds(a, n) for a, n in lay.wide]
    halves = [pl.ds(a, n) for a, n in lay.halves]
    gather, reduce = range(len(wide)), range(len(cols))
    slices = range(max(len(wide), len(cols)))
    first_peers = [(t_peers, y_peers)[h % 2] for h in slices]
    last_peers = [(y_peers, t_peers)[h % 2] for h in slices]
    first_at = [(t, y)[h % 2] for h in slices]
    last_at = [(y, t)[h % 2] for h in slices]

    def yt(h, first_, last_):
        return (last_, first_) if h % 2 == 0 else (first_, last_)

    own = place(p, z, y, t)
    first = pltpu.make_async_copy(tok_in, tok.at[own, :, pl.ds(0, width)], load_sem.at[6])
    small = [pltpu.make_async_copy(ids_in, ids, load_sem.at[7]), pltpu.make_async_copy(rw_in, rw, load_sem.at[8])]
    for load in small:
        load.start()
    first.start()
    loads = [
        pltpu.make_async_copy(src, dst, load_sem.at[i])
        for i, (src, dst) in enumerate(
            ((sg_in, sg), (su_in, su), (wg_in.at[0], wg), (wu_in.at[0], wu), (wd_in.at[0], wd), (sd_in, sd))
        )
    ]
    for load in loads:
        load.start()

    for load in small:
        load.wait()
    lane = lax.broadcasted_iota(jnp.int32, (lay.extra, rows), 0)
    pieces = [jnp.zeros(lane.shape, F32) for _ in range(3)]
    for k in range(ids.shape[0]):
        for m in range(3):
            pieces[m] = pieces[m] + jnp.where(lane == ids[k : k + 1, :] + m * experts, rw[k : k + 1, :], 0.0)
    hi = [v.astype(BF16).astype(F32) for v in pieces]
    rest = [v - h for v, h in zip(pieces, hi)]
    mid = [v.astype(BF16).astype(F32) for v in rest]
    low = [v - h for v, h in zip(rest, mid)]
    mixed = (hi[0] + mid[1] + low[2]).astype(BF16)
    eye = (
        lax.broadcasted_iota(jnp.int32, (rows, rows), 0) == lax.broadcasted_iota(jnp.int32, (rows, rows), 1)
    ).astype(F32).astype(BF16)
    turned = lax.dot_general(eye, mixed, (((1,), (1,)), ((), ())), preferred_element_type=F32)
    tok[own, :, pl.ds(width, lay.extra)] = turned.astype(BF16)

    first.wait()
    beside = jnp.where(z + 1 < nz, 1, 0) + jnp.where(z > 0, 1, 0)
    pl.semaphore_wait(barrier, nt + ny - 1 + beside)

    def remote(src, dst, sem_send, sem_recv, dev):
        return pltpu.make_async_remote_copy(
            src_ref=src, dst_ref=dst, send_sem=sem_send, recv_sem=sem_recv, device_id=dev, device_id_type=MESH)

    def got(view, sem_recv):
        remote(view, view, bulk_send.at[0, 0], sem_recv, partner).wait_recv()

    counts = {}

    def send(kind, h, src, dst, sem_recv, dev, blocks=1):
        remote(src, dst, bulk_send.at[kind, h], sem_recv, dev).start()
        counts[kind, h] = counts.get((kind, h), 0) + blocks

    def send_block(kind, h, idx, sem_recv, dev):
        view = tok.at[idx, :, wide[h]]
        send(kind, h, view, view, sem_recv, dev)

    line_sent = []

    def send_line(slot, idx, z_, target):
        ok = (target >= 0) & (target < nz)
        dev = device(target, y, t)

        def whole():
            remote(tok.at[idx], tok.at[idx], line_send.at[slot], line_recv.at[0, 0], dev).wait_send()

        def part_of(h):
            view = tok.at[idx, :, wide[h]]
            copy = remote(view, view, line_send.at[slot], line_recv.at[h, z_], dev)
            if slot in (0, nz):
                pl.when(ok)(copy.start)
            else:
                copy.start()

        line_sent.append((ok, whole))
        return part_of

    def last_sends(h, idx, z_):
        for v in last_peers[h]:
            send_block(0, h, idx, last_recv.at[h, z_], device(z, *yt(h, first_at[h], v)))

    def swap(h, idx, z_):
        send_block(1, h, idx, swap_recv.at[z_], partner)

    def inner(z_):
        target = jnp.where(z_ < z, z + 1, z - 1)
        return target, (target >= 0) & (target < nz)

    def take(i):
        blk = place(p, seq[i], y, t)
        for h in gather:
            got(tok.at[blk, :, wide[h]], line_recv.at[h, seq[i]])

    def relay_step(i):
        z_ = hops[i]
        target, ok = inner(z_)
        blk = place(p, z_, y, t)
        part_of = send_line(i, blk, z_, target)

        def go():
            for h in gather:
                got(tok.at[blk, :, wide[h]], line_recv.at[h, z_])
                part_of(h)

        pl.when(ok)(go)

    crossing = list(gather)[len(gather) - CROSS :]
    cross_sent = []

    def send_cross(h, slot, z_, target):
        c = h - crossing[0]
        ok = (target >= 0) & (target < nz)
        dev = device(target, y, t)

        def copies():
            for f in first_peers[h]:
                view = tok.at[place(p, z_, *yt(h, f, last_at[h])), :, wide[h]]
                yield remote(view, view, cross_send.at[c, slot], cross_recv.at[c, z_], dev)

        def go():
            for copy in copies():
                copy.start()

        def drained():
            if lay.first[h] > 1:
                view = tok.at[pl.ds(0, lay.first[h] - 1), :, wide[h]]
                remote(view, view, cross_send.at[c, slot], cross_recv.at[c, z_], dev).wait_send()

        cross_sent.append((ok, drained))
        return ok, go

    def start_cross(_):
        for h in crossing:
            for slot, target in ((0, z + 1), (nz, z - 1)):
                ok, start = send_cross(h, slot, z, target)
                pl.when(ok)(start)

    def take_cross(h, z_):
        if lay.first[h] > 1:
            got(tok.at[pl.ds(0, lay.first[h] - 1), :, wide[h]], cross_recv.at[h - crossing[0], z_])

    def relay_cross(k):
        z_ = hops[k]
        target, ok = inner(z_)
        sends = [(h, send_cross(h, k, z_, target)[1]) for h in crossing]

        def go():
            for h, start in sends:
                take_cross(h, z_)
                start()

        pl.when(ok)(go)

    def spread_cross(h, z_):
        for f in first_peers[h]:
            blk = place(p, z_, *yt(h, f, last_at[h]))
            last_sends(h, blk, z_)
            swap(h, blk, z_)

    def inner_cross(i):
        def go():
            for h in crossing:
                spread_cross(h, seq[i])

        pl.when(inner(seq[i])[1])(go)

    def outer_cross(i):
        kept = dict(counts)

        def go():
            for h in crossing:
                take_cross(h, seq[i])
                spread_cross(h, seq[i])

        pl.when(jnp.logical_not(inner(seq[i])[1]))(go)
        counts.clear()
        counts.update(kept)

    def spread(i):
        z_ = seq[i]
        blk = place(p, z_, y, t)
        for h in gather:
            if i and h in crossing:
                continue
            for d, v in enumerate(first_peers[h]):
                send_block(0, h, blk, first_recv.at[h, d * nz + z_], device(z, *yt(h, v, last_at[h])))
        for h in gather:
            last_sends(h, blk, z_)
            swap(h, blk, z_)

    def inner_step(i):
        pl.when(inner(seq[i])[1])(lambda: spread(i))

    def outer_step(i):
        kept = dict(counts)

        def go():
            take(i)
            spread(i)

        pl.when(jnp.logical_not(inner(seq[i])[1]))(go)
        counts.clear()
        counts.update(kept)

    def start_step():
        up, down_ = send_line(0, own, z, z + 1), send_line(nz, own, z, z - 1)
        for h in gather:
            up(h)
            down_(h)
        spread(0)

    def first_step(i):
        z_ = seq[i]
        for h in gather:
            n = lay.first[h]
            if i and h in crossing:
                continue
            onward = h in crossing
            for d in range(n - 1):
                f = (first_at[h] + n - 1 - d) % n
                blk = place(p, z_, *yt(h, f, last_at[h]))
                got(tok.at[blk, :, wide[h]], first_recv.at[h, d * nz + z_])
                if not onward:
                    last_sends(h, blk, z_)
                    swap(h, blk, z_)
            if onward:
                spread_cross(h, z_)

    def last_step(i):
        z_ = seq[i]
        for h in gather:
            n = lay.first[h] * (lay.last[h] - 1)
            if n:
                got(tok.at[pl.ds(0, n), :, wide[h]], last_recv.at[h, z_])
            for f in [first_at[h]] + first_peers[h]:
                for v in last_peers[h]:
                    swap(h, place(p, z_, *yt(h, f, v)), z_)

    def partner_wait(i):
        got(tok.at[pl.ds(place(other, seq[i], 0, 0), chips)], swap_recv.at[seq[i]])

    def hidden_tiles(x, w1, w2, scale, store):
        tile = tile_of(w1.shape[1], 512)
        for n in range(w1.shape[1] // tile):
            at = pl.ds(n * tile, tile)
            g = jnp.dot(x, w1[:, at], preferred_element_type=F32)
            u = jnp.dot(x, w2[:, at], preferred_element_type=F32)
            h = g / (1.0 + jnp.exp(-g)) * u
            if scale is not None:
                h = h * scale
            store[:, at] = h.astype(BF16)

    group = [place(q, z, y, t_) for q in range(2) for t_ in range(nt)]

    def shared_up(_):
        loads[0].wait()
        loads[1].wait()
        x = jnp.concatenate([tok[idx, :, pl.ds(0, width)] for idx in group], axis=0)
        hidden_tiles(x, sg, su, None, hs)

    mine = e_idx * 2 + p

    def up(i):
        if i == 0:
            loads[2].wait()
            loads[3].wait()
        at = pl.ds(seq[i] * lay.plane, lay.plane)
        extra = tok[at, :, pl.ds(width, lay.extra)].reshape(lay.plane * rows, lay.extra)
        l2 = lax.broadcasted_iota(jnp.int32, extra.shape, 1)
        pick = (l2 == mine) | (l2 == mine + experts) | (l2 == mine + 2 * experts)
        scale = jnp.sum(jnp.where(pick, extra.astype(F32), 0.0), axis=1, keepdims=True)
        hidden_tiles(tok[at, :, pl.ds(0, width)].reshape(lay.plane * rows, width), wg, wu, scale, hid)

    def down(i):
        if i == 0:
            loads[4].wait()
            loads[5].wait()
        z_ = seq[i]
        for g, at in enumerate(halves):
            v = jnp.dot(hid[...], wd[:, at], preferred_element_type=F32)
            part[pl.ds(z_ * lay.plane, lay.plane), :, at] = v.astype(BF16).reshape(lay.plane, rows, lay.halves[g][1])
            if i == 0:
                v = jnp.dot(hs[...], sd[:, at], preferred_element_type=F32)
                for j, idx in enumerate(group):
                    part[idx, :, at] = (part[idx, :, at].astype(F32) + v[j * rows : (j + 1) * rows]).astype(BF16)
            send(2, g, part.at[pl.ds(place(other, z_, 0, 0), chips), :, at],
                 recvp.at[pl.ds(z_ * chips, chips), :, at], pair_recv.at[g, z_], partner, chips)

    def buf_b(h, d, z_, f):
        return recvb.at[(d * nz + z_) * lay.first[h] + f, :, cols[h]]

    def buf_a(h, d, z_):
        return recva.at[d * nz + z_, :, cols[h]]

    def add_into(h, idx, others):
        v = part[idx, :, cols[h]].astype(F32)
        for ref in others:
            v = v + ref[...].astype(F32)
        part[idx, :, cols[h]] = v.astype(BF16)

    def mine_of(z_, y_, t_, h):
        return recvp.at[(z_ * ny + y_) * nt + t_, :, cols[h]]

    starts = [0, len(cols) // 2]

    def sums_last(i):
        z_ = seq[i]
        for h in reduce:
            if h in starts:
                g = starts.index(h)
                got(recvp.at[pl.ds(z_ * chips, chips), :, halves[g]], pair_recv.at[g, z_])
            for k, f in enumerate(first_peers[h] + [first_at[h]]):
                here = int(k == lay.first[h] - 1)
                for d, v in enumerate(last_peers[h]):
                    y_, t_ = yt(h, f, v)
                    idx = place(p, z_, y_, t_)
                    add_into(h, idx, [mine_of(z_, y_, t_, h)])
                    send(3, h, part.at[idx, :, cols[h]], buf_b(h, d, z_, f), (a_recv if here else b_recv).at[h, z_],
                         device(z, *yt(h, first_at[h], v)))

    def collect_last(h, z_, f):
        y_, t_ = yt(h, f, last_at[h])
        return place(p, z_, y_, t_), [mine_of(z_, y_, t_, h)] + [buf_b(h, d, z_, f) for d in range(lay.last[h] - 1)]

    def sums_first(i):
        z_ = seq[i]
        for h in reduce:
            n = (lay.first[h] - 1) * (lay.last[h] - 1)
            if n:
                got(recvb.at[pl.ds(0, n), :, cols[h]], b_recv.at[h, z_])
            for d, f in enumerate(first_peers[h]):
                idx, refs = collect_last(h, z_, f)
                add_into(h, idx, refs)
                send(3, h, part.at[idx, :, cols[h]], buf_a(h, d, z_), a_recv.at[h, z_], device(z, *yt(h, f, last_at[h])))

    def sums_line(i):
        z_ = seq[i]
        for h in reduce:
            n = lay.last[h] + lay.first[h] - 2
            if n:
                got(part.at[pl.ds(0, n), :, cols[h]], a_recv.at[h, z_])
            idx, refs = collect_last(h, z_, first_at[h])
            add_into(h, idx, refs + [buf_a(h, d, z_) for d in range(lay.first[h] - 1)])
            if i:
                slot = (z_ - z + nz) % nz - 1
                send(3, h, part.at[idx, :, cols[h]], recvz.at[slot, :, cols[h]], z_recv.at[h], device(z_, y, t))

    start_step()
    steps = {
        "R": relay_step, "X": start_cross, "RB": relay_cross, "Bm": inner_cross, "Be": outer_cross, "A1m": inner_step, "A1e": outer_step, "A2": first_step, "A3": last_step, "W": partner_wait, "S": shared_up, "U": up, "D": down,
        "L": sums_last, "F": sums_first, "Z": sums_line,
    }
    for name, i in schedule(nz):
        steps[name](i)

    stores = []
    for h in reduce:
        if nz > 1:
            got(recvz.at[pl.ds(0, nz - 1), :, cols[h]], z_recv.at[h])
        v = part[own, :, cols[h]].astype(F32)
        for d in range(nz - 1):
            v = v + recvz[d, :, cols[h]].astype(F32)
        result[:, cols[h]] = v.astype(BF16)
        stores.append(pltpu.make_async_copy(result.at[:, cols[h]], out.at[:, cols[h]], store_sem.at[h]))
        stores[-1].start()
    for ok, whole in line_sent + cross_sent:
        pl.when(ok)(whole)
    for (kind, h), n in counts.items():
        view = (tok if kind < 2 else part).at[pl.ds(0, n), :, (wide, wide, halves, cols)[kind][h]]
        remote(view, view, bulk_send.at[kind, h], z_recv.at[h], partner).wait_send()
    for store in stores:
        store.wait()


def per_device(lay, experts, tokens, ids, rw, wg, wu, wd, sg, su, sd):
    rows, width = tokens.shape
    nz, ny, nt = lay.nz, lay.ny, lay.nt
    hidden, shared = wg.shape[2], sg.shape[1]
    n, most = max(GATHER, REDUCE), max(nt, ny)
    many_b = max(1, max((lay.last[h] - 1) * lay.first[h] for h in range(n)) * nz)
    many_a = max(1, (most - 1) * nz)
    anyw = pl.BlockSpec(memory_space=pl.ANY)
    dma = pltpu.SemaphoreType.DMA
    scratch = [
        pltpu.VMEM((lay.blocks, rows, width + lay.extra), BF16),
        pltpu.VMEM((lay.blocks, rows, width), BF16),
        pltpu.VMEM(ids.shape, jnp.int32),
        pltpu.VMEM(rw.shape, F32),
        pltpu.VMEM((lay.blocks // 2, rows, width), BF16),
        pltpu.VMEM((many_b, rows, width), BF16),
        pltpu.VMEM((many_a, rows, width), BF16),
        pltpu.VMEM((max(1, nz - 1), rows, width), BF16),
        pltpu.VMEM((lay.plane * rows, hidden), BF16),
        pltpu.VMEM((2 * nt * rows, shared), BF16),
        pltpu.VMEM(wg.shape[1:], BF16),
        pltpu.VMEM(wu.shape[1:], BF16),
        pltpu.VMEM(wd.shape[1:], BF16),
        pltpu.VMEM(sg.shape, BF16),
        pltpu.VMEM(su.shape, BF16),
        pltpu.VMEM(sd.shape, BF16),
        dma((9,)),
        dma((4, n)),
        dma((nz + 1,)),
        dma((GATHER, nz)),
        dma((GATHER, nz * max(1, most - 1))),
        dma((GATHER, nz)),
        dma((nz,)),
        dma((2, nz)),
        dma((REDUCE, nz)),
        dma((REDUCE, nz)),
        dma((REDUCE,)),
        dma((max(1, CROSS), nz + 1)),
        dma((max(1, CROSS), nz)),
        pltpu.VMEM((rows, width), BF16),
        dma((REDUCE,)),
    ]
    return pl.pallas_call(
        functools.partial(kernel, lay, experts),
        out_shape=jax.ShapeDtypeStruct((rows, width), BF16),
        in_specs=[anyw] * 9,
        out_specs=anyw,
        scratch_shapes=scratch,
        compiler_params=pltpu.CompilerParams(
            collective_id=0, has_side_effects=True, vmem_limit_bytes=67043328
        ),
    )(tokens, ids, rw, wg, wu, wd, sg, su, sd)


def solution(mesh):
    shape = dict(mesh.shape)

    def body(tokens, ids, rw, wg, wu, wd, sg, su, sd):
        experts = shape["expert"] * shape["pair"] * wg.shape[0]
        lay = Layout(shape["expert"], shape["tensor"], tokens.shape[0], tokens.shape[1], experts)
        return per_device(lay, experts, tokens, ids.T, rw.T, wg, wu, wd, sg, su, sd)

    in_specs = (
        P(("groups", "expert", "tensor", "pair"), None),
        P(("groups", "expert", "tensor", "pair"), None),
        P(("groups", "expert", "tensor", "pair"), None),
        P(("expert", "pair"), None, "tensor"),
        P(("expert", "pair"), None, "tensor"),
        P(("expert", "pair"), "tensor", None),
        P(None, ("tensor", "pair")),
        P(None, ("tensor", "pair")),
        P(("tensor", "pair"), None),
    )
    out_specs = P(("groups", "expert", "tensor", "pair"), None)
    return jax.shard_map(body, mesh=mesh, in_specs=in_specs, out_specs=out_specs, check_vma=False)
```
